256 devices in a mesh: lat: 8 (over z), lon: 32 (over x, y, core).
Axes of the slice: x: 4, y: 4, z: 8, core: 2. Of those that a mesh axis runs over, the one named last changes fastest.
Arguments:
- state: float32 [80, 3, 64, 4096], P(None, None, 'lat', 'lon'), may hold values from -6 to 6
- east_courant: float32 [64, 4096], P('lat', 'lon'), may hold values from -0.4 to 0.4
- north_courant: float32 [64, 4096], P('lat', 'lon'), may hold values from -0.4 to 0.4
- obs_cell: int32 [4, 256], replicated, may hold values from 0 to 262143, as said below
- obs_value: float32 [4, 256], replicated, may hold values from -6 to 6
- obs_error_var: float32 [4, 256], replicated, may hold values from 0.25 to 4
- loc_lat: float32 [9], replicated, may hold values from 0.25 to 1
- loc_lon: float32 [129], replicated, may hold values from 0.25 to 1
Outputs:
- analysis: float32 [80, 3, 64, 4096], P(None, None, 'lat', 'lon')
The draws below stay inside these ranges and needn't reach their ends.
Inputs may be any that keep to these rules, and one draw needn't show every extreme that they name: obs_cell holds row * 4096 + column of a cell of the 64 x 4096 grid.
All inputs are finite; a program needn't handle non-finite values.
Results may differ from the reference program's by a relative error of at most 0.0001.
Values sent between devices are 32-bit elements; how exact they have to be, the bound alone decides.
A program may use at most 64 MiB of HBM per device.

```python
import math
import jax
import jax.numpy as jnp
from jax import lax

MEMBERS = 80
FIELDS = 3
LEVELS = 1
BATCHES = 4
NOBS = 256
CLAT = 8
CLON = 128
NLAT = 64
NLON = 4096


def draw_obs_cell(key, part):
    first_key, second_key, third_key = jax.random.split(key, 3)
    tile_cols = NLON // CLON
    tile_count = NLAT // CLAT * tile_cols
    shape = (BATCHES, NOBS)
    tile = jnp.minimum(jax.random.randint(first_key, shape, 0, tile_count), jax.random.randint(second_key, shape, 0, tile_count))
    inside = jax.random.randint(third_key, shape, 0, CLAT * CLON)
    grid_row = tile // tile_cols * CLAT + inside // CLON
    grid_col = tile % tile_cols * CLON + inside % CLON
    return (grid_row * NLON + grid_col).astype(jnp.int32)


def level_of(rng, shape, shards, smallest, top_value):
    loudness, own = 1.0, jax.random.fold_in(rng, 6)
    for position, parts in shards:
        steps = jnp.exp(jax.random.uniform(jax.random.fold_in(own, position), (parts,), jnp.float32, smallest / len(shards), top_value / len(shards)))
        loudness = loudness * jnp.repeat(steps, shape[position] // parts).reshape([-1 if axis == position else 1 for axis in range(len(shape))])
    return loudness


def centred(key, dims, width, limit, cuts=(), held_as=jnp.bfloat16):
    factor_of = level_of(key, dims, cuts, -0.22, 0.18) if cuts else 1.0
    array = jax.random.normal(key, dims, jnp.float32) * width * factor_of
    return jnp.minimum(jnp.maximum(array, -limit), limit).astype(held_as)


def setup_inputs(seed: int = 0) -> dict:
    streams_of = jax.random.split(jax.random.key(seed), 9)
    return {
        "state": centred(streams_of[0], (MEMBERS, FIELDS * LEVELS, NLAT, NLON), 1.0, 6.0, ((2, 8), (3, 32)), jnp.float32),
        "east_courant": jnp.clip(jax.random.uniform(streams_of[1], (NLAT, NLON), jnp.float32, -0.4, 0.4) * level_of(streams_of[1], (NLAT, NLON), ((0, 8), (1, 32)), -0.4, 0.0), -0.4, 0.4),
        "north_courant": jnp.clip(jax.random.uniform(streams_of[2], (NLAT, NLON), jnp.float32, -0.4, 0.4) * level_of(streams_of[2], (NLAT, NLON), ((0, 8), (1, 32)), -0.4, 0.0), -0.4, 0.4),
        "obs_cell": draw_obs_cell(jax.random.fold_in(streams_of[8], 71), 0),
        "obs_value": centred(streams_of[4], (BATCHES, NOBS), 1.0, 6.0, (), jnp.float32),
        "obs_error_var": jnp.clip(jnp.exp(jax.random.uniform(streams_of[5], (BATCHES, NOBS), jnp.float32, math.log(0.25), math.log(4.0))), 0.25, 4.0),
        "loc_lat": jnp.clip(jax.random.uniform(streams_of[6], (CLAT + 1,), jnp.float32, 0.25, 1.0), 0.25, 1.0),
        "loc_lon": jnp.clip(jax.random.uniform(streams_of[7], (CLON + 1,), jnp.float32, 0.25, 1.0), 0.25, 1.0),
    }


diffusion_number = 0.2
variance_eps = 1e-06

def advect(field, east_courant, north_courant):
    east_side = jnp.roll(field, -1, axis=2)
    west_side = jnp.roll(field, 1, axis=2)
    zero_row = jnp.zeros_like(field[:, :1])
    north_side = jnp.concatenate([field[:, 1:], zero_row], axis=1)
    south_side = jnp.concatenate([zero_row, field[:, :-1]], axis=1)
    return field - 0.5 * east_courant * (east_side - west_side) - 0.5 * north_courant * (north_side - south_side) + diffusion_number * (east_side + west_side + north_side + south_side - 4.0 * field)

def obs_increments(priors, values, error_var):
    prior_mean = lax.optimization_barrier(jnp.mean(priors, axis=0))
    anomaly = priors - prior_mean
    variance = lax.optimization_barrier(jnp.sum(anomaly * anomaly, axis=0)) / (MEMBERS - 1) + variance_eps
    post_var = 1.0 / (1.0 / variance + 1.0 / error_var)
    post_mean = post_var * (prior_mean / variance + values / error_var)
    return (anomaly, variance, post_mean + jnp.sqrt(post_var / variance) * anomaly - priors)

def regress(field, anomaly, variance, increments, lat_obs, lon_obs, window_weights):
    field_anom = field - lax.optimization_barrier(jnp.mean(field, axis=0))
    padded = jnp.pad(field_anom, ((0, 0), (CLAT, CLAT), (0, 0)))
    padded = jnp.concatenate([padded[:, :, NLON - CLON:], padded, padded[:, :, :CLON]], axis=2)
    start_acc = jnp.zeros_like(padded)

    def step(accum, item):
        obs_anom, obs_inc, obs_var, row_start, col_start = item
        anchor = jnp.zeros((), jnp.int32)
        window = lax.dynamic_slice(padded, (anchor, row_start, col_start), (MEMBERS, 2 * CLAT + 1, 2 * CLON + 1))
        covar = jnp.einsum('m,mij->ij', obs_anom, window, precision=lax.Precision.HIGHEST) / (MEMBERS - 1)
        gain = covar * window_weights / obs_var
        region = lax.dynamic_slice(accum, (anchor, row_start, col_start), (MEMBERS, 2 * CLAT + 1, 2 * CLON + 1))
        region = region + obs_inc[:, None, None] * gain[None]
        return (lax.dynamic_update_slice(accum, region, (anchor, row_start, col_start)), None)
    accum, _ = lax.scan(step, start_acc, (anomaly.T, increments.T, variance, lat_obs.astype(jnp.int32), lon_obs.astype(jnp.int32)))
    inner = accum[:, CLAT:CLAT + NLAT, :]
    core = inner[:, :, CLON:CLON + NLON]
    core = core.at[:, :, NLON - CLON:].add(inner[:, :, :CLON])
    core = core.at[:, :, :CLON].add(inner[:, :, CLON + NLON:])
    return field + core

def reference(state, east_courant, north_courant, obs_cell, obs_value, obs_error_var, loc_lat, loc_lon):
    fields = [advect(state[:, index], east_courant, north_courant) for index in range(FIELDS * LEVELS)]
    lat_profile = jnp.concatenate([loc_lat[::-1], loc_lat[1:]])
    lon_profile = jnp.concatenate([loc_lon[::-1], loc_lon[1:]])
    window_weights = lat_profile[:, None] * lon_profile[None, :]
    for batch_index in range(BATCHES):
        cells = obs_cell[batch_index]
        lat_obs = cells // NLON
        lon_obs = cells % NLON
        priors = fields[0].reshape(MEMBERS, NLAT * NLON)[:, cells]
        anomaly, variance, increments = obs_increments(priors, obs_value[batch_index], obs_error_var[batch_index])
        fields = [regress(field, anomaly, variance, increments, lat_obs, lon_obs, window_weights) for field in fields]
    return jnp.stack(fields, axis=1)
```

```python
import jax
import jax.numpy as jnp
from jax import lax
from jax.sharding import PartitionSpec as P

diffusion_number = 0.2
variance_eps = 1e-06
highest = lax.Precision.HIGHEST


def shifted(value, axis, by, closed):
    count = lax.axis_size(axis)
    pairs = [(i, (i + by) % count) for i in range(count) if closed or 0 <= i + by < count]
    return lax.ppermute(value, axis, pairs)


def padded(cells, axis, dim, closed):
    last = cells.shape[dim] - 1
    head = lax.slice_in_dim(cells, 0, 1, axis=dim)
    tail = lax.slice_in_dim(cells, last, last + 1, axis=dim)
    return jnp.concatenate(
        [shifted(tail, axis, 1, closed), cells, shifted(head, axis, -1, closed)], axis=dim
    )


def obs_increments(priors, values, error_var, members):
    prior_mean = jnp.mean(priors, axis=0)
    anomaly = priors - prior_mean
    variance = jnp.sum(anomaly * anomaly, axis=0) / (members - 1) + variance_eps
    post_var = 1.0 / (1.0 / variance + 1.0 / error_var)
    post_mean = post_var * (prior_mean / variance + values / error_var)
    return (anomaly, variance, post_mean + jnp.sqrt(post_var / variance) * anomaly - priors)


def collect(local_priors):
    column = (
        local_priors
        + shifted(local_priors, "lat", 1, False)
        + shifted(local_priors, "lat", -1, False)
    )
    return column + shifted(column, "lon", 1, True) + shifted(column, "lon", -1, True)


def looked_up(table, distance):
    steps = jnp.arange(table.shape[0], dtype=jnp.int32)[:, None, None]
    return jnp.sum(jnp.where(distance[None] == steps, table[:, None, None], 0.0), axis=0)


def general(
    state, east_courant, north_courant, obs_cell, obs_value, obs_error_var, loc_lat, loc_lon
):
    members, channels, tile_rows, tile_cols = state.shape
    cell_count = tile_rows * tile_cols
    batches, obs_count = obs_cell.shape
    lat_padded = padded(state, "lat", 2, False)
    lon_padded = padded(state, "lon", 3, True)
    north_side = lat_padded[:, :, 2:, :]
    south_side = lat_padded[:, :, :-2, :]
    east_side = lon_padded[:, :, :, 2:]
    west_side = lon_padded[:, :, :, :-2]
    advected = (
        state
        - 0.5 * east_courant * (east_side - west_side)
        - 0.5 * north_courant * (north_side - south_side)
        + diffusion_number * (east_side + west_side + north_side + south_side - 4.0 * state)
    )
    first_row = lax.axis_index("lat") * tile_rows
    first_col = lax.axis_index("lon") * tile_cols
    grid_cols = tile_cols * lax.axis_size("lon")
    row_ids = first_row + jnp.arange(tile_rows, dtype=jnp.int32)
    col_ids = first_col + jnp.arange(tile_cols, dtype=jnp.int32)

    def step(batch, field):
        cells = lax.dynamic_index_in_dim(obs_cell, batch, 0, False)
        values = lax.dynamic_index_in_dim(obs_value, batch, 0, False)
        error_var = lax.dynamic_index_in_dim(obs_error_var, batch, 0, False)
        obs_row, obs_col = cells // grid_cols, cells % grid_cols
        spot = (obs_row - first_row) * tile_cols + obs_col - first_col
        owned = (obs_col >= first_col) & (obs_col < first_col + tile_cols)
        spot = jnp.where(owned, spot, -1)
        chosen = (jnp.arange(cell_count, dtype=jnp.int32)[:, None] == spot[None, :]).astype(
            jnp.float32
        )
        priors = collect(jnp.dot(field[:, :cell_count], chosen, precision=highest))
        lat_dist = jnp.abs(row_ids[None, :] - obs_row[:, None])
        gap = (col_ids[None, :] - obs_col[:, None]) % grid_cols
        lon_dist = jnp.minimum(gap, grid_cols - gap)
        weights = (
            looked_up(loc_lat, lat_dist)[:, :, None] * looked_up(loc_lon, lon_dist)[:, None, :]
        ).reshape(obs_count, cell_count)
        anomaly, variance, increments = obs_increments(priors, values, error_var, members)
        field_anom = field - jnp.mean(field, axis=0)
        covar = lax.dot_general(
            anomaly, field_anom, (((0,), (0,)), ((), ())), precision=highest
        ) / (members - 1)
        gain = covar * jnp.tile(weights, (1, channels)) / variance[:, None]
        return field + jnp.dot(increments, gain, precision=highest)

    field = lax.fori_loop(0, batches, step, advected.reshape(members, channels * cell_count))
    return field.reshape(state.shape)


def solution(mesh):
    in_specs = (
        P(None, None, "lat", "lon"),
        P("lat", "lon"),
        P("lat", "lon"),
        P(),
        P(),
        P(),
        P(),
        P(),
    )
    out_specs = P(None, None, "lat", "lon")
    return jax.shard_map(
        general, mesh=mesh, in_specs=in_specs, out_specs=out_specs, check_vma=False
    )
```

```python
import functools
import jax
import jax.numpy as jnp
from jax import lax
from jax.experimental import pallas as pl
from jax.experimental.pallas import tpu as pltpu
from jax.sharding import PartitionSpec as P

diffusion_number = 0.2
variance_eps = 1e-06
highest = lax.Precision.HIGHEST
mesh_ids = pl.DeviceIdType.MESH

rows, cols, lats, lons = 8, 128, 8, 32
members, channels, batches, batch_obs = 80, 3, 4, 256
tile_room, room = 24, 24
reach = 4


def shifted(value, axis, by, closed):
    count = lax.axis_size(axis)
    pairs = [(i, (i + by) % count) for i in range(count) if closed or 0 <= i + by < count]
    return lax.ppermute(value, axis, pairs)


def padded(cells, axis, dim, closed):
    last = cells.shape[dim] - 1
    head = lax.slice_in_dim(cells, 0, 1, axis=dim)
    tail = lax.slice_in_dim(cells, last, last + 1, axis=dim)
    return jnp.concatenate(
        [shifted(tail, axis, 1, closed), cells, shifted(head, axis, -1, closed)], axis=dim
    )


def obs_increments(priors, values, error_var):
    prior_mean = jnp.mean(priors, axis=0)
    anomaly = priors - prior_mean
    variance = jnp.sum(anomaly * anomaly, axis=0) / (members - 1) + variance_eps
    post_var = 1.0 / (1.0 / variance + 1.0 / error_var)
    post_mean = post_var * (prior_mean / variance + values / error_var)
    return (anomaly, variance, post_mean + jnp.sqrt(post_var / variance) * anomaly - priors)


def collect(local_priors):
    column = (
        local_priors
        + shifted(local_priors, "lat", 1, False)
        + shifted(local_priors, "lat", -1, False)
    )
    return column + shifted(column, "lon", 1, True) + shifted(column, "lon", -1, True)


def looked_up(table, distance):
    steps = jnp.arange(table.shape[0], dtype=jnp.int32)[:, None, None]
    return jnp.sum(jnp.where(distance[None] == steps, table[:, None, None], 0.0), axis=0)


def general(
    state, east_courant, north_courant, obs_cell, obs_value, obs_error_var, loc_lat, loc_lon
):
    tile_rows, tile_cols = state.shape[2:]
    cell_count = tile_rows * tile_cols
    obs_count = obs_cell.shape[1]
    lat_padded = padded(state, "lat", 2, False)
    lon_padded = padded(state, "lon", 3, True)
    north_side = lat_padded[:, :, 2:, :]
    south_side = lat_padded[:, :, :-2, :]
    east_side = lon_padded[:, :, :, 2:]
    west_side = lon_padded[:, :, :, :-2]
    advected = (
        state
        - 0.5 * east_courant * (east_side - west_side)
        - 0.5 * north_courant * (north_side - south_side)
        + diffusion_number * (east_side + west_side + north_side + south_side - 4.0 * state)
    )
    first_row = lax.axis_index("lat") * tile_rows
    first_col = lax.axis_index("lon") * tile_cols
    grid_cols = tile_cols * lax.axis_size("lon")
    row_ids = first_row + jnp.arange(tile_rows, dtype=jnp.int32)
    col_ids = first_col + jnp.arange(tile_cols, dtype=jnp.int32)

    def step(batch, field):
        cells = lax.dynamic_index_in_dim(obs_cell, batch, 0, False)
        values = lax.dynamic_index_in_dim(obs_value, batch, 0, False)
        error_var = lax.dynamic_index_in_dim(obs_error_var, batch, 0, False)
        obs_row, obs_col = cells // grid_cols, cells % grid_cols
        spot = (obs_row - first_row) * tile_cols + obs_col - first_col
        owned = (obs_col >= first_col) & (obs_col < first_col + tile_cols)
        spot = jnp.where(owned, spot, -1)
        chosen = (jnp.arange(cell_count, dtype=jnp.int32)[:, None] == spot[None, :]).astype(
            jnp.float32
        )
        priors = collect(jnp.dot(field[:, :cell_count], chosen, precision=highest))
        lat_dist = jnp.abs(row_ids[None, :] - obs_row[:, None])
        gap = (col_ids[None, :] - obs_col[:, None]) % grid_cols
        lon_dist = jnp.minimum(gap, grid_cols - gap)
        weights = (
            looked_up(loc_lat, lat_dist)[:, :, None] * looked_up(loc_lon, lon_dist)[:, None, :]
        ).reshape(obs_count, cell_count)
        anomaly, variance, increments = obs_increments(priors, values, error_var)
        field_anom = field - jnp.mean(field, axis=0)
        covar = lax.dot_general(
            anomaly, field_anom, (((0,), (0,)), ((), ())), precision=highest
        ) / (members - 1)
        gain = covar * jnp.tile(weights, (1, channels)) / variance[:, None]
        return field + jnp.dot(increments, gain, precision=highest)

    field = lax.fori_loop(0, batches, step, advected.reshape(members, channels * cell_count))
    return field.reshape(state.shape)


def iota(shape, dim):
    return lax.broadcasted_iota(jnp.int32, shape, dim)


def one_hot(condition):
    return condition.astype(jnp.float32)


def dot_t(a, b, precision=None):
    return lax.dot_general(
        a, b, (((1,), (1,)), ((), ())), precision=precision, preferred_element_type=jnp.float32
    )


def earlier_counts(marks):
    size = marks.shape[1]
    earlier = (iota((size, size), 0) < iota((size, size), 1)).astype(jnp.bfloat16)
    return jnp.dot(marks.astype(jnp.bfloat16), earlier, preferred_element_type=jnp.float32)


def place(cells):
    return cells >> 15, (cells >> 12) & 7, (cells >> 7) & 31, cells & 127


def advect_row(here, north, south, west_halo, east_halo, east_courant, north_courant):
    lane = iota(here.shape, 1)
    east = jnp.where(lane == cols - 1, east_halo, pltpu.roll(here, cols - 1, 1))
    west = jnp.where(lane == 0, west_halo, pltpu.roll(here, 1, 1))
    return (
        here
        - 0.5 * east_courant * (east - west)
        - 0.5 * north_courant * (north - south)
        + diffusion_number * (east + west + north + south - 4.0 * here)
    )


def exchange_kernel(
    state, east_courant, north_courant, obs_cell, adv_out, prior_out,
    cells_in, from_north, from_south, edge_out, edge_in, lat_own, lat_in, col_own, lon_in,
    load_sem, halo_send, halo_recv, lat_send, lat_recv, lon_send, lon_recv,
):
    la, lo = lax.axis_index("lat"), lax.axis_index("lon")

    def at(dlat, dlon):
        return ((la + dlat) & (lats - 1), (lo + dlon) & (lons - 1))

    lat_steps = [1, 7, 2, 6, 3, 5, 4]
    lon_steps = [1, -1, 2, -2, 3, -3, 4, -4]
    barrier = pltpu.get_barrier_semaphore()
    loads = [
        [
            pltpu.make_async_copy(
                state.at[:, k, r, :], cells_in.at[k * rows + r], load_sem.at[k * rows + r]
            )
            for r in range(rows)
        ]
        for k in range(channels)
    ]
    for k in range(channels):
        for load in loads[k]:
            load.start()
    peers = [at(1, 0), at(-1, 0), at(0, 1), at(0, -1)]
    peers += [at(d, 0) for d in lat_steps[2:]] + [at(0, d) for d in lon_steps[2:]]
    for peer in peers:
        pl.semaphore_signal(barrier, inc=1, device_id=peer, device_id_type=mesh_ids)
    lat_own[...] = jnp.zeros_like(lat_own)
    lane = iota((members, cols), 1)

    def pack_edges(k):
        for side, column in ((0, 0), (1, cols - 1)):
            packed = jnp.zeros((members, cols), jnp.float32)
            for r in range(rows):
                edge = cells_in[k * rows + r, :, column : column + 1]
                packed = jnp.where(lane == r, edge, packed)
            edge_out[side, k] = packed

    def halo_copies(first, count, base):
        made = []
        sends = [
            (cells_in.at[first * rows], from_north.at[first], at(-1, 0)),
            (cells_in.at[first * rows + rows - 1], from_south.at[first], at(1, 0)),
            (edge_out.at[1, first], edge_in.at[0, first], at(0, 1)),
            (edge_out.at[0, first], edge_in.at[1, first], at(0, -1)),
        ]
        for i, (src, dst, peer) in enumerate(sends):
            made.append(
                pltpu.make_async_remote_copy(
                    src_ref=src, dst_ref=dst, send_sem=halo_send.at[base + i],
                    recv_sem=halo_recv.at[base + i], device_id=peer, device_id_type=mesh_ids,
                )
            )
        return made

    for load in loads[0]:
        load.wait()
    pack_edges(0)
    pl.semaphore_wait(barrier, len(peers))
    halos = [halo_copies(k, 1, 4 * k) for k in range(channels)]
    for copy in halos[0]:
        copy.start()
    for k in range(1, channels):
        for load in loads[k]:
            load.wait()
        pack_edges(k)
        for copy in halos[k]:
            copy.start()

    lat_tile, row, lon_tile, col = place(obs_cell[...])
    mine = [lon_tile[b : b + 1] == lo for b in range(batches)]
    tile = (la - iota((lats, batch_obs), 0)) & (lats - 1)
    marks = [one_hot((lat_tile[b : b + 1] == tile) & mine[b]) for b in range(batches)]
    counts = earlier_counts(jnp.concatenate(marks, axis=0))
    base = jnp.zeros((lats, 1), jnp.float32)
    tile_slot, col_slot = [], []
    for b in range(batches):
        before = counts[b * lats : (b + 1) * lats]
        tile_slot.append(jnp.where(marks[b] > 0, before + base, -1.0))
        col_slot.append(jnp.where(mine[b], jnp.sum(before, axis=0, keepdims=True), -1.0))
        base = base + jnp.sum(marks[b], axis=1, keepdims=True)
    slot_ids = iota((tile_room, batch_obs), 0).astype(jnp.float32)
    in_slot = [
        [one_hot(tile_slot[b][d : d + 1] == slot_ids).astype(jnp.bfloat16) for d in range(lats)]
        for b in range(batches)
    ]
    found = jnp.zeros((tile_room, 8), jnp.float32)
    for b in range(batches):
        kinds = iota((8, batch_obs), 0)
        facts = jnp.where(
            kinds == 0,
            row[b : b + 1],
            jnp.where(kinds == 1, col[b : b + 1], jnp.where(kinds == 2, 1, 0)),
        ).astype(jnp.float32).astype(jnp.bfloat16)
        found = found + dot_t(in_slot[b][0], facts)
    slot_row = jnp.where(found[:, 2:3] > 0.5, found[:, 0:1], -1.0)
    slot_col = found[:, 1:2]

    def advect(k):
        no_north, no_south = la == lats - 1, la == 0
        for r in range(rows):
            here = cells_in[k * rows + r]
            if r + 1 < rows:
                north = cells_in[k * rows + r + 1]
            else:
                north = jnp.where(no_north, 0.0, from_north[k])
            if r > 0:
                south = cells_in[k * rows + r - 1]
            else:
                south = jnp.where(no_south, 0.0, from_south[k])
            adv_out[k * rows + r] = advect_row(
                here, north, south, edge_in[0, k, :, r : r + 1], edge_in[1, k, :, r : r + 1],
                east_courant[r : r + 1, :], north_courant[r : r + 1, :],
            )

    for copy in halos[0]:
        copy.wait_recv()
    advect(0)
    spot = iota((tile_room, cols), 1).astype(jnp.float32)
    picked = jnp.zeros((tile_room, members), jnp.float32)
    for r in range(rows):
        chosen = one_hot((slot_col == spot) & (slot_row == r))
        picked = picked + dot_t(chosen, adv_out[r], highest)
    lat_own[:, :members] = picked
    lat_copies = []
    for d in lat_steps:
        copy = pltpu.make_async_remote_copy(
            src_ref=lat_own, dst_ref=lat_in.at[d - 1], send_sem=lat_send.at[d - 1],
            recv_sem=lat_recv.at[d - 1], device_id=at(d, 0), device_id_type=mesh_ids,
        )
        copy.start()
        lat_copies.append(copy)

    col_ids = iota((room, batch_obs), 0).astype(jnp.float32)
    moves = []
    for b in range(batches):
        wanted = one_hot(col_slot[b] == col_ids).astype(jnp.bfloat16)
        moves.append(dot_t(wanted, jnp.concatenate(in_slot[b], axis=0)))
    move = jnp.concatenate(moves, axis=0)
    for k in range(1, channels):
        for copy in halos[k]:
            copy.wait_recv()
        advect(k)
    for copy in lat_copies:
        copy.wait_recv()
    parts = jnp.concatenate([lat_own[...]] + [lat_in[d] for d in range(lats - 1)], axis=0)
    column = jnp.dot(move, parts, precision=highest, preferred_element_type=jnp.float32)
    col_own[...] = column
    lon_copies = []
    for i, d in enumerate(lon_steps):
        size = room * (reach + 1 - abs(d))
        size = min(size, room * batches)
        copy = pltpu.make_async_remote_copy(
            src_ref=col_own.at[pl.ds(0, size)], dst_ref=lon_in.at[reach - d, pl.ds(0, size)],
            send_sem=lon_send.at[i], recv_sem=lon_recv.at[i],
            device_id=at(0, d), device_id_type=mesh_ids,
        )
        copy.start()
        lon_copies.append(copy)
    prior_out[reach] = column
    for i, d in enumerate(lon_steps):
        lon_copies[i].wait_recv()
    for d in lon_steps:
        size = min(room * (reach + 1 - abs(d)), room * batches)
        prior_out[reach - d, :size] = lon_in[reach - d, :size]
        if size < room * batches:
            prior_out[reach - d, size:] = jnp.zeros((room * batches - size, cols), jnp.float32)
    for copies in (*halos, lat_copies, lon_copies):
        for copy in copies:
            copy.wait_send()


def exchange(state, east_courant, north_courant, obs_cell):
    vmem = pl.BlockSpec(memory_space=pltpu.VMEM)
    f32 = jnp.float32
    slots = room * batches
    return pl.pallas_call(
        exchange_kernel,
        name="exchange",
        out_shape=(
            jax.ShapeDtypeStruct((channels * rows, members, cols), f32),
            jax.ShapeDtypeStruct((2 * reach + 1, slots, cols), f32),
        ),
        in_specs=[pl.BlockSpec(memory_space=pl.ANY), vmem, vmem, vmem],
        out_specs=(vmem, vmem),
        scratch_shapes=[
            pltpu.VMEM((channels * rows, members, cols), f32),
            pltpu.VMEM((channels, members, cols), f32),
            pltpu.VMEM((channels, members, cols), f32),
            pltpu.VMEM((2, channels, members, cols), f32),
            pltpu.VMEM((2, channels, members, cols), f32),
            pltpu.VMEM((tile_room, cols), f32),
            pltpu.VMEM((lats - 1, tile_room, cols), f32),
            pltpu.VMEM((slots, cols), f32),
            pltpu.VMEM((2 * reach + 1, slots, cols), f32),
            pltpu.SemaphoreType.DMA((channels * rows,)),
            pltpu.SemaphoreType.DMA((4 * channels,)),
            pltpu.SemaphoreType.DMA((4 * channels,)),
            pltpu.SemaphoreType.DMA((lats - 1,)),
            pltpu.SemaphoreType.DMA((lats - 1,)),
            pltpu.SemaphoreType.DMA((2 * reach,)),
            pltpu.SemaphoreType.DMA((2 * reach,)),
        ],
        compiler_params=pltpu.CompilerParams(
            collective_id=0, has_side_effects=True, vmem_limit_bytes=24 << 20
        ),
    )(state, east_courant, north_courant, obs_cell)


def update_kernel(
    adv, priors, obs_cell, obs_value, obs_error_var, loc_lat, loc_lon, out, field, slots, sem
):
    la, lo = lax.axis_index("lat"), lax.axis_index("lon")
    lat_tile, row, lon_tile, col = place(obs_cell[...])
    values, errors = obs_value[...], obs_error_var[...]
    slots[...] = priors[...]

    distance = jnp.abs(iota((cols * 2, 4 * cols), 1) - 2 * cols)
    table = one_hot(distance == iota((cols * 2, 4 * cols), 0))
    ends = one_hot(jnp.abs(iota((8, 4 * cols), 1) - 2 * cols) == cols)
    line = jnp.dot(
        jnp.broadcast_to(loc_lon[:, :cols], (8, cols)), table[:cols], precision=highest,
        preferred_element_type=jnp.float32,
    ) + ends * loc_lon[:, cols : cols + 1]
    shifted_lines = pltpu.roll(
        jnp.broadcast_to(line[0:1], (cols, 4 * cols)), 0, 1, stride=1, stride_axis=0
    )
    lon_table = shifted_lines[:, cols:]

    def lat_weight(gap):
        weight = jnp.zeros(gap.shape, jnp.float32)
        for d in range(rows + 1):
            weight = jnp.where(jnp.abs(gap) == d, loc_lat[d], weight)
        return weight

    lane = iota((1, cols), 1)
    spans = [reach - b for b in range(batches)]
    slot_ids = iota((room, batch_obs), 0).astype(jnp.float32)
    col_of, row_of, value_of, error_of, lon_of, col_hot, row_hot, lat_of = ([] for _ in range(8))
    tiles = (lo - reach + iota((16, batch_obs), 0)) & (lons - 1)
    marks = [one_hot(lon_tile[b : b + 1] == tiles) for b in range(batches)]
    counts = earlier_counts(jnp.concatenate(marks, axis=0))
    for b in range(batches):
        taken = jnp.where(marks[b] > 0, counts[16 * b : 16 * b + 16], -1.0)
        hot = jnp.concatenate(
            [
                one_hot(taken[reach + k : reach + k + 1] == slot_ids)
                for k in range(-spans[b], spans[b] + 1)
            ],
            axis=0,
        )
        kinds = iota((8, batch_obs), 0)
        whole_row = (lat_tile[b : b + 1] * rows + row[b : b + 1]).astype(jnp.float32)
        facts = jnp.where(kinds == 0, col[b : b + 1].astype(jnp.float32), 0.0)
        facts = jnp.where(kinds == 1, whole_row, facts)
        facts = jnp.where(kinds == 2, values[b : b + 1], facts)
        facts = jnp.where(kinds == 3, errors[b : b + 1], facts)
        facts = jnp.where(kinds == 4, 1.0, facts)
        found = dot_t(hot, facts, highest)
        valid = found[:, 4:5] > 0.5
        where_col = jnp.where(valid, found[:, 0:1], -1.0).astype(jnp.int32)
        where_row = found[:, 1:2].astype(jnp.int32)
        value_of.append(found[:, 2:3])
        error_of.append(jnp.where(valid, found[:, 3:4], 1.0))
        row_of.append(where_row)
        col_hot.append(one_hot(where_col == lane))
        row_hot.append(one_hot(where_row == lane))
        lon_of.append(
            jnp.dot(
                col_hot[b], lon_table, precision=highest, preferred_element_type=jnp.float32
            )
        )
        lat_of.append(lat_weight(where_row - lane))

    def block(b, k):
        first = (k + spans[b]) * room
        return slice(first, first + room)

    def lon_field(b, k):
        return jnp.concatenate(
            [
                lon_of[b][block(b, k - 1), 2 * cols : 3 * cols],
                lon_of[b][block(b, k), cols : 2 * cols],
                lon_of[b][block(b, k + 1), :cols],
            ],
            axis=0,
        )

    def around(k, b):
        first = (k - 1 + spans[b]) * room
        return slice(first, first + 3 * room)

    later = {}
    for b in range(batches - 1):
        for k in range(-spans[b] + 1, spans[b]):
            targets = [c for c in range(b + 1, batches) if abs(k) <= spans[c]]
            cols_t = jnp.concatenate([col_hot[c][block(c, k)] for c in targets], axis=0)
            rows_t = jnp.concatenate([row_hot[c][block(c, k)] for c in targets], axis=0)
            later[b, k] = dot_t(lon_field(b, k), cols_t, highest) * dot_t(
                lat_of[b][around(k, b)], rows_t, highest
            )

    is_member = lane < members
    chunk = 4
    copies = []
    for b in range(batches):
        mine = slice(b * room, (b + 1) * room)
        prior = jnp.concatenate(
            [slots[reach + k, mine] for k in range(-spans[b], spans[b] + 1)], axis=0
        )
        mean = jnp.sum(prior, axis=1, keepdims=True) / members
        anomaly = jnp.where(is_member, prior - mean, 0.0)
        variance = (
            jnp.sum(anomaly * anomaly, axis=1, keepdims=True) / (members - 1) + variance_eps
        )
        post_var = 1.0 / (1.0 / variance + 1.0 / error_of[b])
        post_mean = post_var * (mean / variance + value_of[b] / error_of[b])
        increment = post_mean + jnp.sqrt(post_var / variance) * anomaly - prior
        increment = jnp.where(is_member, increment, 0.0)
        scaled = anomaly / ((members - 1) * variance)
        for k in range(-spans[b] + 1, spans[b]):
            if (b, k) not in later:
                continue
            first = (b + 1) * room
            size = later[b, k].shape[1]
            target = slots[reach + k, first : first + size]
            gain = dot_t(scaled[around(k, b)], target, highest) * later[b, k]
            slots[reach + k, first : first + size] = target + lax.dot_general(
                gain, increment[around(k, b)], (((0,), (0,)), ((), ())), precision=highest,
                preferred_element_type=jnp.float32,
            )
        near = around(0, b)
        weights = lon_field(b, 0)
        here_scaled, here_increment = scaled[near, :members], increment[near, :members]
        by_row = [
            lat_weight(row_of[b][near] - (la * rows + r)) * weights for r in range(rows)
        ]
        before = adv if b == 0 else field
        for start in range(0, channels * rows, chunk):
            cells = jnp.concatenate([before[start + i] for i in range(chunk)], axis=1)
            covar = jnp.dot(
                here_scaled, cells, precision=highest, preferred_element_type=jnp.float32
            )
            gain = covar * jnp.concatenate(
                [by_row[(start + i) % rows] for i in range(chunk)], axis=1
            )
            cells = cells + lax.dot_general(
                here_increment, gain, (((0,), (0,)), ((), ())), precision=highest,
                preferred_element_type=jnp.float32,
            )
            for i in range(chunk):
                field[start + i] = cells[:, i * cols : (i + 1) * cols]
                if b == batches - 1:
                    k, r = divmod(start + i, rows)
                    copy = pltpu.make_async_copy(field.at[start + i], out.at[:, k, r, :], sem.at[start + i])
                    copy.start()
                    copies.append(copy)
    for copy in copies:
        copy.wait()


def update(adv, priors, obs_cell, obs_value, obs_error_var, loc_lat, loc_lon):
    vmem = pl.BlockSpec(memory_space=pltpu.VMEM)
    smem = pl.BlockSpec(memory_space=pltpu.SMEM)
    return pl.pallas_call(
        update_kernel,
        name="update",
        out_shape=jax.ShapeDtypeStruct((members, channels, rows, cols), jnp.float32),
        in_specs=[vmem] * 5 + [smem, vmem],
        out_specs=pl.BlockSpec(memory_space=pl.ANY),
        scratch_shapes=[
            pltpu.VMEM((channels * rows, members, cols), jnp.float32),
            pltpu.VMEM((2 * reach + 1, room * batches, cols), jnp.float32),
            pltpu.SemaphoreType.DMA((channels * rows,)),
        ],
        compiler_params=pltpu.CompilerParams(vmem_limit_bytes=32 << 20),
    )(adv, priors, obs_cell, obs_value, obs_error_var, loc_lat, loc_lon.reshape(1, -1))


def fast(
    state, east_courant, north_courant, obs_cell, obs_value, obs_error_var, loc_lat, loc_lon
):
    adv, priors = exchange(state, east_courant, north_courant, obs_cell)
    return update(adv, priors, obs_cell, obs_value, obs_error_var, loc_lat, loc_lon)


def fits(obs_cell):
    lat_tile, _, lon_tile, _ = place(obs_cell)
    tile = lat_tile * lons + lon_tile
    in_tile = jnp.sum(
        (tile.reshape(-1)[:, None] == jnp.arange(lats * lons)[None, :]).astype(jnp.int32), axis=0
    )
    in_column = jnp.sum(
        (lon_tile[:, :, None] == jnp.arange(lons)[None, None, :]).astype(jnp.int32), axis=1
    )
    return (jnp.max(in_tile) <= tile_room) & (jnp.max(in_column) <= room)


def on_device(*args):
    return lax.cond(fits(args[3]), fast, general, *args)


def solution(mesh):
    in_specs = (
        P(None, None, "lat", "lon"),
        P("lat", "lon"),
        P("lat", "lon"),
        P(),
        P(),
        P(),
        P(),
        P(),
    )
    out_specs = P(None, None, "lat", "lon")
    return jax.shard_map(
        on_device, mesh=mesh, in_specs=in_specs, out_specs=out_specs, check_vma=False
    )
```

```python
import functools
import jax
import jax.numpy as jnp
from jax import lax
from jax.experimental import pallas as pl
from jax.experimental.pallas import tpu as pltpu
from jax.sharding import PartitionSpec as P

diffusion_number = 0.2
variance_eps = 1e-06
highest = lax.Precision.HIGHEST
mesh_ids = pl.DeviceIdType.MESH

rows, cols, lats, lons = 8, 128, 8, 32
members, channels, batches, batch_obs = 80, 3, 4, 256
tile_room, room = 24, 24
reach = 4


def shifted(value, axis, by, closed):
    count = lax.axis_size(axis)
    pairs = [(i, (i + by) % count) for i in range(count) if closed or 0 <= i + by < count]
    return lax.ppermute(value, axis, pairs)


def padded(cells, axis, dim, closed):
    last = cells.shape[dim] - 1
    head = lax.slice_in_dim(cells, 0, 1, axis=dim)
    tail = lax.slice_in_dim(cells, last, last + 1, axis=dim)
    return jnp.concatenate(
        [shifted(tail, axis, 1, closed), cells, shifted(head, axis, -1, closed)], axis=dim
    )


def obs_increments(priors, values, error_var):
    prior_mean = jnp.mean(priors, axis=0)
    anomaly = priors - prior_mean
    variance = jnp.sum(anomaly * anomaly, axis=0) / (members - 1) + variance_eps
    post_var = 1.0 / (1.0 / variance + 1.0 / error_var)
    post_mean = post_var * (prior_mean / variance + values / error_var)
    return (anomaly, variance, post_mean + jnp.sqrt(post_var / variance) * anomaly - priors)


def collect(local_priors):
    column = (
        local_priors
        + shifted(local_priors, "lat", 1, False)
        + shifted(local_priors, "lat", -1, False)
    )
    return column + shifted(column, "lon", 1, True) + shifted(column, "lon", -1, True)


def looked_up(table, distance):
    steps = jnp.arange(table.shape[0], dtype=jnp.int32)[:, None, None]
    return jnp.sum(jnp.where(distance[None] == steps, table[:, None, None], 0.0), axis=0)


def general(
    state, east_courant, north_courant, obs_cell, obs_value, obs_error_var, loc_lat, loc_lon
):
    tile_rows, tile_cols = state.shape[2:]
    cell_count = tile_rows * tile_cols
    obs_count = obs_cell.shape[1]
    lat_padded = padded(state, "lat", 2, False)
    lon_padded = padded(state, "lon", 3, True)
    north_side = lat_padded[:, :, 2:, :]
    south_side = lat_padded[:, :, :-2, :]
    east_side = lon_padded[:, :, :, 2:]
    west_side = lon_padded[:, :, :, :-2]
    advected = (
        state
        - 0.5 * east_courant * (east_side - west_side)
        - 0.5 * north_courant * (north_side - south_side)
        + diffusion_number * (east_side + west_side + north_side + south_side - 4.0 * state)
    )
    first_row = lax.axis_index("lat") * tile_rows
    first_col = lax.axis_index("lon") * tile_cols
    grid_cols = tile_cols * lax.axis_size("lon")
    row_ids = first_row + jnp.arange(tile_rows, dtype=jnp.int32)
    col_ids = first_col + jnp.arange(tile_cols, dtype=jnp.int32)

    def step(batch, field):
        cells = lax.dynamic_index_in_dim(obs_cell, batch, 0, False)
        values = lax.dynamic_index_in_dim(obs_value, batch, 0, False)
        error_var = lax.dynamic_index_in_dim(obs_error_var, batch, 0, False)
        obs_row, obs_col = cells // grid_cols, cells % grid_cols
        spot = (obs_row - first_row) * tile_cols + obs_col - first_col
        owned = (obs_col >= first_col) & (obs_col < first_col + tile_cols)
        spot = jnp.where(owned, spot, -1)
        chosen = (jnp.arange(cell_count, dtype=jnp.int32)[:, None] == spot[None, :]).astype(
            jnp.float32
        )
        priors = collect(jnp.dot(field[:, :cell_count], chosen, precision=highest))
        lat_dist = jnp.abs(row_ids[None, :] - obs_row[:, None])
        gap = (col_ids[None, :] - obs_col[:, None]) % grid_cols
        lon_dist = jnp.minimum(gap, grid_cols - gap)
        weights = (
            looked_up(loc_lat, lat_dist)[:, :, None] * looked_up(loc_lon, lon_dist)[:, None, :]
        ).reshape(obs_count, cell_count)
        anomaly, variance, increments = obs_increments(priors, values, error_var)
        field_anom = field - jnp.mean(field, axis=0)
        covar = lax.dot_general(
            anomaly, field_anom, (((0,), (0,)), ((), ())), precision=highest
        ) / (members - 1)
        gain = covar * jnp.tile(weights, (1, channels)) / variance[:, None]
        return field + jnp.dot(increments, gain, precision=highest)

    field = lax.fori_loop(0, batches, step, advected.reshape(members, channels * cell_count))
    return field.reshape(state.shape)


def iota(shape, dim):
    return lax.broadcasted_iota(jnp.int32, shape, dim)


def one_hot(condition):
    return condition.astype(jnp.float32)


def dot_t(a, b, precision=None):
    return lax.dot_general(
        a, b, (((1,), (1,)), ((), ())), precision=precision, preferred_element_type=jnp.float32
    )


def dot(a, b):
    return jnp.dot(a, b, preferred_element_type=jnp.float32)


def halves(value):
    high = value.astype(jnp.bfloat16).astype(jnp.float32)
    return high, value - high


def earlier_counts(marks):
    size = marks.shape[1]
    earlier = (iota((size, size), 0) < iota((size, size), 1)).astype(jnp.bfloat16)
    return jnp.dot(marks.astype(jnp.bfloat16), earlier, preferred_element_type=jnp.float32)


def place(cells):
    return cells >> 15, (cells >> 12) & 7, (cells >> 7) & 31, cells & 127


spans = [reach - b for b in range(batches)]


def block(b, k):
    first = (k + spans[b]) * room
    return slice(first, first + room)


def around(k, b):
    first = (k - 1 + spans[b]) * room
    return slice(first, first + 3 * room)


def rows_of(b):
    first = sum(2 * spans[c] + 1 for c in range(b)) * room
    return slice(first, first + (2 * spans[b] + 1) * room)


def targets(b):
    return range(-spans[b] + 1, spans[b]) if b + 1 < batches else ()


def later_batches(b, k):
    return [c for c in range(b + 1, batches) if abs(k) <= spans[c]]


def pair_rows(b, k):
    return room * len(later_batches(b, k))


pair_ids = {
    pair: i for i, pair in enumerate((b, k) for b in range(batches) for k in targets(b))
}


def lat_weight(gap, loc_lat):
    weight = jnp.zeros(gap.shape, jnp.float32)
    for d in range(rows + 1):
        weight = jnp.where(jnp.abs(gap) == d, loc_lat[d], weight)
    return weight


def column_weights(loc_lon):
    wide = (2 * cols, 4 * cols)
    distance = jnp.abs(iota(wide, 1) - 2 * cols)
    table = one_hot(distance == iota(wide, 0))[:cols]
    ends = one_hot(jnp.abs(iota((8, 4 * cols), 1) - 2 * cols) == cols)
    line = jnp.dot(
        jnp.broadcast_to(loc_lon[:, :cols], (8, cols)), table, precision=highest,
        preferred_element_type=jnp.float32,
    ) + ends * loc_lon[:, cols : cols + 1]
    lines = jnp.broadcast_to(line[0:1], (cols, 4 * cols))
    return pltpu.roll(lines, 0, 1, stride=1, stride_axis=0)[:, cols:]


def advect_row(here, north, south, west_halo, east_halo, east_courant, north_courant):
    lane = iota(here.shape, 1)
    east = jnp.where(lane == cols - 1, east_halo, pltpu.roll(here, cols - 1, 1))
    west = jnp.where(lane == 0, west_halo, pltpu.roll(here, 1, 1))
    return (
        here
        - 0.5 * east_courant * (east - west)
        - 0.5 * north_courant * (north - south)
        + diffusion_number * (east + west + north + south - 4.0 * here)
    )


def exchange_kernel(
    state, east_courant_in, north_courant_in, obs_cell_in, obs_value_in, obs_error_var_in,
    loc_lat, loc_lon_in, adv_out, prior_out, obs_terms, pair_weights, cell_weights, overflow,
    east_courant, north_courant, obs_cell, obs_value, obs_error_var, loc_lon, small_sem,
    cells_in, from_north, from_south, edge_out, edge_in, lat_own, lat_in, col_own, lon_in,
    load_sem, halo_send, halo_recv, lat_send, lat_recv, lon_send, lon_recv,
):
    la, lo = lax.axis_index("lat"), lax.axis_index("lon")

    def at(dlat, dlon):
        return ((la + dlat) & (lats - 1), (lo + dlon) & (lons - 1))

    lat_steps = [1, 7, 2, 6, 3, 5, 4]
    lon_steps = [1, -1, 2, -2, 3, -3, 4, -4]
    barrier = pltpu.get_barrier_semaphore()
    loads = [
        [
            pltpu.make_async_copy(
                state.at[:, k, r, :], cells_in.at[k * rows + r], load_sem.at[k * rows + r]
            )
            for r in range(rows)
        ]
        for k in range(channels)
    ]
    pairs = [
        (obs_cell_in, obs_cell), (east_courant_in, east_courant),
        (north_courant_in, north_courant), (obs_value_in, obs_value),
        (obs_error_var_in, obs_error_var), (loc_lon_in, loc_lon),
    ]
    small = [
        pltpu.make_async_copy(src, dst, small_sem.at[i]) for i, (src, dst) in enumerate(pairs)
    ]
    for load in loads[0] + small + loads[1] + loads[2]:
        load.start()
    peers = [at(1, 0), at(-1, 0), at(0, 1), at(0, -1)]
    peers += [at(d, 0) for d in lat_steps[2:]] + [at(0, d) for d in lon_steps[2:]]
    for peer in peers:
        pl.semaphore_signal(barrier, inc=1, device_id=peer, device_id_type=mesh_ids)
    lat_own[...] = jnp.zeros_like(lat_own)
    lane = iota((members, cols), 1)

    def pack_edges(k):
        for side, column in ((0, 0), (1, cols - 1)):
            packed = jnp.zeros((members, cols), jnp.float32)
            for r in range(rows):
                edge = cells_in[k * rows + r, :, column : column + 1]
                packed = jnp.where(lane == r, edge, packed)
            edge_out[side, k] = packed

    def halo_copies(first, count, base):
        made = []
        sends = [
            (cells_in.at[first * rows], from_north.at[first], at(-1, 0)),
            (cells_in.at[first * rows + rows - 1], from_south.at[first], at(1, 0)),
            (edge_out.at[1, first], edge_in.at[0, first], at(0, 1)),
            (edge_out.at[0, first], edge_in.at[1, first], at(0, -1)),
        ]
        for i, (src, dst, peer) in enumerate(sends):
            made.append(
                pltpu.make_async_remote_copy(
                    src_ref=src, dst_ref=dst, send_sem=halo_send.at[base + i],
                    recv_sem=halo_recv.at[base + i], device_id=peer, device_id_type=mesh_ids,
                )
            )
        return made

    for load in loads[0]:
        load.wait()
    pack_edges(0)
    pl.semaphore_wait(barrier, len(peers))
    halos = [halo_copies(k, 1, 4 * k) for k in range(channels)]
    for copy in halos[0]:
        copy.start()
    for k in range(1, channels):
        for load in loads[k]:
            load.wait()
        pack_edges(k)
        for copy in halos[k]:
            copy.start()

    for load in small:
        load.wait()

    lat_tile, row, lon_tile, col = place(obs_cell[...])
    mine = [lon_tile[b : b + 1] == lo for b in range(batches)]
    tile = (la - iota((lats, batch_obs), 0)) & (lats - 1)
    marks = [one_hot((lat_tile[b : b + 1] == tile) & mine[b]) for b in range(batches)]
    counts = earlier_counts(jnp.concatenate(marks, axis=0))
    base = jnp.zeros((lats, 1), jnp.float32)
    tile_slot, col_slot = [], []
    for b in range(batches):
        before = counts[b * lats : (b + 1) * lats]
        tile_slot.append(jnp.where(marks[b] > 0, before + base, -1.0))
        col_slot.append(jnp.where(mine[b], jnp.sum(before, axis=0, keepdims=True), -1.0))
        base = base + jnp.sum(marks[b], axis=1, keepdims=True)
    slot_ids = iota((tile_room, batch_obs), 0).astype(jnp.float32)
    in_slot = [
        [one_hot(tile_slot[b][d : d + 1] == slot_ids).astype(jnp.bfloat16) for d in range(lats)]
        for b in range(batches)
    ]
    found = jnp.zeros((tile_room, 8), jnp.float32)
    for b in range(batches):
        kinds = iota((8, batch_obs), 0)
        facts = jnp.where(
            kinds == 0,
            row[b : b + 1],
            jnp.where(kinds == 1, col[b : b + 1], jnp.where(kinds == 2, 1, 0)),
        ).astype(jnp.float32).astype(jnp.bfloat16)
        found = found + dot_t(in_slot[b][0], facts)
    slot_row = jnp.where(found[:, 2:3] > 0.5, found[:, 0:1], -1.0)
    slot_col = found[:, 1:2]

    def advect(k):
        no_north, no_south = la == lats - 1, la == 0
        for r in range(rows):
            here = cells_in[k * rows + r]
            if r + 1 < rows:
                north = cells_in[k * rows + r + 1]
            else:
                north = jnp.where(no_north, 0.0, from_north[k])
            if r > 0:
                south = cells_in[k * rows + r - 1]
            else:
                south = jnp.where(no_south, 0.0, from_south[k])
            adv_out[k * rows + r] = advect_row(
                here, north, south, edge_in[0, k, :, r : r + 1], edge_in[1, k, :, r : r + 1],
                east_courant[r : r + 1, :], north_courant[r : r + 1, :],
            )

    for copy in halos[0]:
        copy.wait_recv()
    advect(0)
    spot = iota((tile_room, cols), 1).astype(jnp.float32)
    picked = jnp.zeros((tile_room, members), jnp.float32)
    for r in range(rows):
        chosen = one_hot((slot_col == spot) & (slot_row == r))
        picked = picked + dot_t(chosen, adv_out[r], highest)
    lat_own[:, :members] = picked
    lat_copies = []
    for d in lat_steps:
        copy = pltpu.make_async_remote_copy(
            src_ref=lat_own, dst_ref=lat_in.at[d - 1], send_sem=lat_send.at[d - 1],
            recv_sem=lat_recv.at[d - 1], device_id=at(d, 0), device_id_type=mesh_ids,
        )
        copy.start()
        lat_copies.append(copy)

    col_ids = iota((room, batch_obs), 0).astype(jnp.float32)
    moves = []
    for b in range(batches):
        wanted = one_hot(col_slot[b] == col_ids).astype(jnp.bfloat16)
        moves.append(dot_t(wanted, jnp.concatenate(in_slot[b], axis=0)))
    move = jnp.concatenate(moves, axis=0)
    for k in range(1, channels):
        for copy in halos[k]:
            copy.wait_recv()
        advect(k)

    inverse_error = 1.0 / obs_error_var[...]
    value_term = obs_value[...] * inverse_error
    lon_table = column_weights(loc_lon)
    lanes = iota((1, cols), 1)
    tiles = (lo - reach + iota((16, batch_obs), 0)) & (lons - 1)
    marks = [one_hot(lon_tile[b : b + 1] == tiles) for b in range(batches)]
    counts = earlier_counts(jnp.concatenate(marks, axis=0))
    row_ids, lon_of, col_hot, row_hot, lat_of = [], [], [], [], []
    kinds = iota((8, batch_obs), 0)
    for b in range(batches):
        taken = jnp.where(marks[b] > 0, counts[16 * b : 16 * b + 16], -1.0)
        hot = jnp.concatenate(
            [
                one_hot(taken[reach + k : reach + k + 1] == slot_ids)
                for k in range(-spans[b], spans[b] + 1)
            ],
            axis=0,
        )
        one = slice(b, b + 1)
        whole_row = (lat_tile[one] * rows + row[one]).astype(jnp.float32)
        facts = jnp.where(kinds == 0, inverse_error[one], 0.0)
        facts = jnp.where(kinds == 1, value_term[one], facts)
        facts = jnp.where(kinds == 2, col[one].astype(jnp.float32), facts)
        facts = jnp.where(kinds == 3, whole_row, facts)
        facts = jnp.where(kinds == 4, 1.0, facts)
        found = dot_t(hot, facts, highest)
        obs_terms[rows_of(b), :] = found
        at_col = jnp.where(found[:, 4:5] > 0.5, found[:, 2:3], -1.0).astype(jnp.int32)
        at_row = found[:, 3:4].astype(jnp.int32)
        row_ids.append(at_row)
        col_hot.append(one_hot(at_col == lanes))
        row_hot.append(one_hot(at_row == lanes))
        lon_of.append(
            jnp.dot(
                col_hot[b], lon_table, precision=highest, preferred_element_type=jnp.float32
            )
        )
        lat_of.append(lat_weight(at_row - lanes, loc_lat))

    def lon_field(b, k):
        return jnp.concatenate(
            [
                lon_of[b][block(b, k - 1), 2 * cols : 3 * cols],
                lon_of[b][block(b, k), cols : 2 * cols],
                lon_of[b][block(b, k + 1), :cols],
            ],
            axis=0,
        )

    unused = jnp.zeros((cols - 3 * room, cols), jnp.float32)

    for copy in lat_copies:
        copy.wait_recv()
    parts = jnp.concatenate([lat_own[...]] + [lat_in[d] for d in range(lats - 1)], axis=0)
    column = jnp.dot(move, parts, precision=highest, preferred_element_type=jnp.float32)
    col_own[...] = column
    lon_copies = []
    for i, d in enumerate(lon_steps):
        size = room * (reach + 1 - abs(d))
        size = min(size, room * batches)
        copy = pltpu.make_async_remote_copy(
            src_ref=col_own.at[pl.ds(0, size)], dst_ref=lon_in.at[reach - d, pl.ds(0, size)],
            send_sem=lon_send.at[i], recv_sem=lon_recv.at[i],
            device_id=at(0, d), device_id_type=mesh_ids,
        )
        copy.start()
        lon_copies.append(copy)
    prior_out[reach] = column

    for (b, k), i in pair_ids.items():
        later = later_batches(b, k)
        cols_t = jnp.concatenate([col_hot[c][block(c, k)] for c in later], axis=0)
        rows_t = jnp.concatenate([row_hot[c][block(c, k)] for c in later], axis=0)
        by_lon = jnp.concatenate([lon_field(b, k), unused], axis=0)
        by_lat = jnp.concatenate([lat_of[b][around(k, b)], unused], axis=0)
        pair_weights[i, : pair_rows(b, k)] = dot_t(cols_t, by_lon, highest) * dot_t(
            rows_t, by_lat, highest
        )
    for b in range(batches):
        weights = lon_field(b, 0)
        for r in range(rows):
            gap = row_ids[b][around(0, b)] - (la * rows + r)
            cell_weights[b, r] = lat_weight(gap, loc_lat) * weights
    in_tile = jnp.zeros((lats, lons), jnp.float32)
    too_many = jnp.zeros((1, lons), jnp.float32)
    for b in range(batches):
        by_lat = one_hot(lat_tile[b : b + 1] == iota((lats, batch_obs), 0))
        by_lon = one_hot(lon_tile[b : b + 1] == iota((lons, batch_obs), 0))
        tally = dot_t(by_lat.astype(jnp.bfloat16), by_lon.astype(jnp.bfloat16))
        in_tile = in_tile + tally
        too_many = jnp.maximum(too_many, jnp.sum(tally, axis=0, keepdims=True) - room)
    too_many = jnp.maximum(too_many, jnp.max(in_tile, axis=0, keepdims=True) - tile_room)
    overflow[0, 0] = jnp.max(too_many).astype(jnp.int32)
    for i, d in enumerate(lon_steps):
        lon_copies[i].wait_recv()
    for d in lon_steps:
        size = min(room * (reach + 1 - abs(d)), room * batches)
        prior_out[reach - d, :size] = lon_in[reach - d, :size]
        if size < room * batches:
            prior_out[reach - d, size:] = jnp.zeros((room * batches - size, cols), jnp.float32)
    for copies in (*halos, lat_copies, lon_copies):
        for copy in copies:
            copy.wait_send()


def exchange(
    state, east_courant, north_courant, obs_cell, obs_value, obs_error_var, loc_lat, loc_lon
):
    vmem = pl.BlockSpec(memory_space=pltpu.VMEM)
    smem = pl.BlockSpec(memory_space=pltpu.SMEM)
    f32 = jnp.float32
    slots = room * batches
    return pl.pallas_call(
        exchange_kernel,
        name="exchange",
        out_shape=(
            jax.ShapeDtypeStruct((channels * rows, members, cols), f32),
            jax.ShapeDtypeStruct((2 * reach + 1, slots, cols), f32),
            jax.ShapeDtypeStruct((rows_of(batches - 1).stop, 8), f32),
            jax.ShapeDtypeStruct((len(pair_ids), 3 * room, cols), f32),
            jax.ShapeDtypeStruct((batches, rows, 3 * room, cols), f32),
            jax.ShapeDtypeStruct((1, 1), jnp.int32),
        ),
        in_specs=[pl.BlockSpec(memory_space=pltpu.HBM)] * 6 + [smem, pl.BlockSpec(memory_space=pltpu.HBM)],
        out_specs=(vmem,) * 5 + (smem,),
        scratch_shapes=[
            pltpu.VMEM((rows, cols), f32),
            pltpu.VMEM((rows, cols), f32),
            pltpu.VMEM((batches, batch_obs), jnp.int32),
            pltpu.VMEM((batches, batch_obs), f32),
            pltpu.VMEM((batches, batch_obs), f32),
            pltpu.VMEM((1, cols + 1), f32),
            pltpu.SemaphoreType.DMA((6,)),
            pltpu.VMEM((channels * rows, members, cols), f32),
            pltpu.VMEM((channels, members, cols), f32),
            pltpu.VMEM((channels, members, cols), f32),
            pltpu.VMEM((2, channels, members, cols), f32),
            pltpu.VMEM((2, channels, members, cols), f32),
            pltpu.VMEM((tile_room, cols), f32),
            pltpu.VMEM((lats - 1, tile_room, cols), f32),
            pltpu.VMEM((slots, cols), f32),
            pltpu.VMEM((2 * reach + 1, slots, cols), f32),
            pltpu.SemaphoreType.DMA((channels * rows,)),
            pltpu.SemaphoreType.DMA((4 * channels,)),
            pltpu.SemaphoreType.DMA((4 * channels,)),
            pltpu.SemaphoreType.DMA((lats - 1,)),
            pltpu.SemaphoreType.DMA((lats - 1,)),
            pltpu.SemaphoreType.DMA((2 * reach,)),
            pltpu.SemaphoreType.DMA((2 * reach,)),
        ],
        compiler_params=pltpu.CompilerParams(
            collective_id=0, has_side_effects=True, vmem_limit_bytes=24 << 20
        ),
    )(
        state, east_courant, north_courant, obs_cell, obs_value, obs_error_var, loc_lat,
        loc_lon.reshape(1, -1),
    )


def update_kernel(adv, priors, obs_terms, pair_weights, cell_weights, out, field, slots, sem):
    slots[...] = priors[...]
    lane = iota((1, cols), 1)
    is_member = lane < members
    unused = jnp.zeros((cols - 3 * room, cols), jnp.float32)
    unused_three = jnp.zeros((cols - 3 * room, 3 * cols), jnp.float32)
    chunk = 4
    copies = []
    for b in range(batches):
        mine = slice(b * room, (b + 1) * room)
        prior = jnp.concatenate(
            [slots[reach + k, mine] for k in range(-spans[b], spans[b] + 1)], axis=0
        )
        mean = jnp.sum(prior, axis=1, keepdims=True) / members
        anomaly = jnp.where(is_member, prior - mean, 0.0)
        variance = (
            jnp.sum(anomaly * anomaly, axis=1, keepdims=True) / (members - 1) + variance_eps
        )
        precision = 1.0 / variance
        post_var = 1.0 / (precision + obs_terms[rows_of(b), 0:1])
        post_mean = post_var * (mean * precision + obs_terms[rows_of(b), 1:2])
        increment = post_mean + jnp.sqrt(post_var * precision) * anomaly - prior
        increment = jnp.where(is_member, increment, 0.0)
        scaled = anomaly * (precision / (members - 1))
        increment_high, increment_low = halves(increment)
        scaled_high, scaled_low = halves(scaled)
        scaled_three = jnp.concatenate([scaled_high, scaled_high, scaled_low], axis=1)
        for k in targets(b):
            first = (b + 1) * room
            size = pair_rows(b, k)
            target = slots[reach + k, first : first + size]
            high, low = halves(target)
            target_three = jnp.concatenate([high, low, high], axis=1).astype(jnp.bfloat16)
            sources = jnp.concatenate([scaled_three[around(k, b)], unused_three], axis=0)
            gain = dot_t(target_three, sources.astype(jnp.bfloat16))
            high, low = halves(gain * pair_weights[pair_ids[b, k], :size])
            gain_three = jnp.concatenate([high, low, high], axis=1).astype(jnp.bfloat16)
            near_high = jnp.concatenate([increment_high[around(k, b)], unused], axis=0)
            near_low = jnp.concatenate([increment_low[around(k, b)], unused], axis=0)
            near_three = jnp.concatenate([near_high, near_high, near_low], axis=0)
            slots[reach + k, first : first + size] = target + dot(
                gain_three, near_three.astype(jnp.bfloat16)
            )
        near = around(0, b)
        none = jnp.zeros((3 * room, cols), jnp.float32)
        high = jnp.concatenate([scaled_high[near], none], axis=1)
        low = jnp.concatenate([scaled_low[near], none], axis=1)
        scaled_by_member = (
            high + pltpu.roll(high, members, 1) + pltpu.roll(low, 2 * members, 1)
        ).astype(jnp.bfloat16)
        increment_by_slot = jnp.concatenate(
            [
                increment_high[near],
                increment_high[near],
                increment_low[near],
                jnp.zeros((2 * cols - 9 * room, cols), jnp.float32),
            ],
            axis=0,
        )
        increment_by_slot = increment_by_slot.T[:members].astype(jnp.bfloat16)
        before = adv if b == 0 else field
        for start in range(0, channels * rows, chunk):
            cells = jnp.concatenate([before[start + i] for i in range(chunk)], axis=1)
            high = cells.astype(jnp.bfloat16)
            low = (cells - high.astype(jnp.float32)).astype(jnp.bfloat16)
            three = jnp.concatenate(
                [high, low, high, jnp.zeros((2 * cols - 3 * members, chunk * cols), jnp.bfloat16)],
                axis=0,
            )
            gain = dot(scaled_by_member, three) * jnp.concatenate(
                [cell_weights[b, (start + i) % rows] for i in range(chunk)], axis=1
            )
            high, low = halves(gain)
            three = jnp.concatenate(
                [high, low, high, jnp.zeros((2 * cols - 9 * room, chunk * cols), jnp.float32)],
                axis=0,
            ).astype(jnp.bfloat16)
            cells = cells + dot(increment_by_slot, three)
            for i in range(chunk):
                field[start + i] = cells[:, i * cols : (i + 1) * cols]
                if b == batches - 1:
                    k, r = divmod(start + i, rows)
                    copy = pltpu.make_async_copy(
                        field.at[start + i], out.at[:, k, r, :], sem.at[start + i]
                    )
                    copy.start()
                    copies.append(copy)
    for copy in copies:
        copy.wait()


def update(*operands):
    vmem = pl.BlockSpec(memory_space=pltpu.VMEM)
    return pl.pallas_call(
        update_kernel,
        name="update",
        out_shape=jax.ShapeDtypeStruct((members, channels, rows, cols), jnp.float32),
        in_specs=[vmem] * 5,
        out_specs=pl.BlockSpec(memory_space=pltpu.HBM),
        scratch_shapes=[
            pltpu.VMEM((channels * rows, members, cols), jnp.float32),
            pltpu.VMEM((2 * reach + 1, room * batches, cols), jnp.float32),
            pltpu.SemaphoreType.DMA((channels * rows,)),
        ],
        compiler_params=pltpu.CompilerParams(vmem_limit_bytes=32 << 20),
    )(*operands)


def on_device(*args):
    *operands, overflow = exchange(*args)
    return lax.cond(
        overflow.reshape(()) > 0,
        lambda args, operands: general(*args),
        lambda args, operands: update(*operands),
        args,
        tuple(operands),
    )


def solution(mesh):
    in_specs = (
        P(None, None, "lat", "lon"),
        P("lat", "lon"),
        P("lat", "lon"),
        P(),
        P(),
        P(),
        P(),
        P(),
    )
    out_specs = P(None, None, "lat", "lon")
    return jax.shard_map(
        on_device, mesh=mesh, in_specs=in_specs, out_specs=out_specs, check_vma=False
    )
```

```python
import functools
import jax
import jax.numpy as jnp
from jax import lax
from jax.experimental import pallas as pl
from jax.experimental.pallas import tpu as pltpu
from jax.sharding import PartitionSpec as P

diffusion_number = 0.2
variance_eps = 1e-06
highest = lax.Precision.HIGHEST
mesh_ids = pl.DeviceIdType.MESH

rows, cols, lats, lons = 8, 128, 8, 32
members, channels, batches, batch_obs = 80, 3, 4, 256
tile_room, room, packed_room = 24, 24, 16
reach = 4


def shifted(value, axis, by, closed):
    count = lax.axis_size(axis)
    pairs = [(i, (i + by) % count) for i in range(count) if closed or 0 <= i + by < count]
    return lax.ppermute(value, axis, pairs)


def padded(cells, axis, dim, closed):
    last = cells.shape[dim] - 1
    head = lax.slice_in_dim(cells, 0, 1, axis=dim)
    tail = lax.slice_in_dim(cells, last, last + 1, axis=dim)
    return jnp.concatenate(
        [shifted(tail, axis, 1, closed), cells, shifted(head, axis, -1, closed)], axis=dim
    )


def obs_increments(priors, values, error_var):
    prior_mean = jnp.mean(priors, axis=0)
    anomaly = priors - prior_mean
    variance = jnp.sum(anomaly * anomaly, axis=0) / (members - 1) + variance_eps
    post_var = 1.0 / (1.0 / variance + 1.0 / error_var)
    post_mean = post_var * (prior_mean / variance + values / error_var)
    return (anomaly, variance, post_mean + jnp.sqrt(post_var / variance) * anomaly - priors)


def collect(local_priors):
    column = (
        local_priors
        + shifted(local_priors, "lat", 1, False)
        + shifted(local_priors, "lat", -1, False)
    )
    return column + shifted(column, "lon", 1, True) + shifted(column, "lon", -1, True)


def looked_up(table, distance):
    steps = jnp.arange(table.shape[0], dtype=jnp.int32)[:, None, None]
    return jnp.sum(jnp.where(distance[None] == steps, table[:, None, None], 0.0), axis=0)


def general(
    state, east_courant, north_courant, obs_cell, obs_value, obs_error_var, loc_lat, loc_lon
):
    tile_rows, tile_cols = state.shape[2:]
    cell_count = tile_rows * tile_cols
    obs_count = obs_cell.shape[1]
    lat_padded = padded(state, "lat", 2, False)
    lon_padded = padded(state, "lon", 3, True)
    north_side = lat_padded[:, :, 2:, :]
    south_side = lat_padded[:, :, :-2, :]
    east_side = lon_padded[:, :, :, 2:]
    west_side = lon_padded[:, :, :, :-2]
    advected = (
        state
        - 0.5 * east_courant * (east_side - west_side)
        - 0.5 * north_courant * (north_side - south_side)
        + diffusion_number * (east_side + west_side + north_side + south_side - 4.0 * state)
    )
    first_row = lax.axis_index("lat") * tile_rows
    first_col = lax.axis_index("lon") * tile_cols
    grid_cols = tile_cols * lax.axis_size("lon")
    row_ids = first_row + jnp.arange(tile_rows, dtype=jnp.int32)
    col_ids = first_col + jnp.arange(tile_cols, dtype=jnp.int32)

    def step(batch, field):
        cells = lax.dynamic_index_in_dim(obs_cell, batch, 0, False)
        values = lax.dynamic_index_in_dim(obs_value, batch, 0, False)
        error_var = lax.dynamic_index_in_dim(obs_error_var, batch, 0, False)
        obs_row, obs_col = cells // grid_cols, cells % grid_cols
        spot = (obs_row - first_row) * tile_cols + obs_col - first_col
        owned = (obs_col >= first_col) & (obs_col < first_col + tile_cols)
        spot = jnp.where(owned, spot, -1)
        chosen = (jnp.arange(cell_count, dtype=jnp.int32)[:, None] == spot[None, :]).astype(
            jnp.float32
        )
        priors = collect(jnp.dot(field[:, :cell_count], chosen, precision=highest))
        lat_dist = jnp.abs(row_ids[None, :] - obs_row[:, None])
        gap = (col_ids[None, :] - obs_col[:, None]) % grid_cols
        lon_dist = jnp.minimum(gap, grid_cols - gap)
        weights = (
            looked_up(loc_lat, lat_dist)[:, :, None] * looked_up(loc_lon, lon_dist)[:, None, :]
        ).reshape(obs_count, cell_count)
        anomaly, variance, increments = obs_increments(priors, values, error_var)
        field_anom = field - jnp.mean(field, axis=0)
        covar = lax.dot_general(
            anomaly, field_anom, (((0,), (0,)), ((), ())), precision=highest
        ) / (members - 1)
        gain = covar * jnp.tile(weights, (1, channels)) / variance[:, None]
        return field + jnp.dot(increments, gain, precision=highest)

    field = lax.fori_loop(0, batches, step, advected.reshape(members, channels * cell_count))
    return field.reshape(state.shape)


def iota(shape, dim):
    return lax.broadcasted_iota(jnp.int32, shape, dim)


def one_hot(condition):
    return condition.astype(jnp.float32)


def dot_t(a, b, precision=None):
    return lax.dot_general(
        a, b, (((1,), (1,)), ((), ())), precision=precision, preferred_element_type=jnp.float32
    )


def dot(a, b):
    return jnp.dot(a, b, preferred_element_type=jnp.float32)


def halves(value):
    high = value.astype(jnp.bfloat16).astype(jnp.float32)
    return high, value - high


def earlier_counts(marks):
    size = marks.shape[1]
    earlier = (iota((size, size), 0) < iota((size, size), 1)).astype(jnp.bfloat16)
    return jnp.dot(marks.astype(jnp.bfloat16), earlier, preferred_element_type=jnp.float32)


def place(cells):
    return cells >> 15, (cells >> 12) & 7, (cells >> 7) & 31, cells & 127


spans = [reach - b for b in range(batches)]


def block(b, k):
    first = (k + spans[b]) * room
    return slice(first, first + room)


def around(k, b):
    first = (k - 1 + spans[b]) * room
    return slice(first, first + 3 * room)


def rows_of(b):
    first = sum(2 * spans[c] + 1 for c in range(b)) * room
    return slice(first, first + (2 * spans[b] + 1) * room)


def targets(b):
    return range(-spans[b] + 1, spans[b]) if b + 1 < batches else ()


def later_batches(b, k):
    return [c for c in range(b + 1, batches) if abs(k) <= spans[c]]


def pair_rows(b, k):
    return room * len(later_batches(b, k))


pair_ids = {
    pair: i for i, pair in enumerate((b, k) for b in range(batches) for k in targets(b))
}


def lat_weight(gap, loc_lat):
    weight = jnp.zeros(gap.shape, jnp.float32)
    for d in range(rows + 1):
        weight = jnp.where(jnp.abs(gap) == d, loc_lat[d], weight)
    return weight


def column_weights(loc_lon):
    wide = (2 * cols, 4 * cols)
    distance = jnp.abs(iota(wide, 1) - 2 * cols)
    table = one_hot(distance == iota(wide, 0))[:cols]
    ends = one_hot(jnp.abs(iota((8, 4 * cols), 1) - 2 * cols) == cols)
    line = jnp.dot(
        jnp.broadcast_to(loc_lon[:, :cols], (8, cols)), table, precision=highest,
        preferred_element_type=jnp.float32,
    ) + ends * loc_lon[:, cols : cols + 1]
    lines = jnp.broadcast_to(line[0:1], (cols, 4 * cols))
    return pltpu.roll(lines, 0, 1, stride=1, stride_axis=0)[:, cols:]


def packed(block):
    lane = iota((8, cols), 1)
    last = block[16:24]
    return jnp.concatenate(
        [
            jnp.where(lane < members, block[:8], pltpu.roll(last, members, 1)),
            jnp.where(lane < members, block[8:16], pltpu.roll(last, 32, 1)),
        ],
        axis=0,
    )


def unpacked(block):
    lane = iota((8, cols), 1)
    first, second = block[:8], block[8:16]
    last = jnp.where(lane < 48, pltpu.roll(first, 48, 1), pltpu.roll(second, 96, 1))
    three = [jnp.where(lane < members, part, 0.0) for part in (first, second, last)]
    return jnp.concatenate(three, axis=0)


def advect_row(here, north, south, west_halo, east_halo, east_courant, north_courant):
    lane = iota(here.shape, 1)
    east = jnp.where(lane == cols - 1, east_halo, pltpu.roll(here, cols - 1, 1))
    west = jnp.where(lane == 0, west_halo, pltpu.roll(here, 1, 1))
    return (
        here
        - 0.5 * east_courant * (east - west)
        - 0.5 * north_courant * (north - south)
        + diffusion_number * (east + west + north + south - 4.0 * here)
    )


def exchange_kernel(
    state, east_courant_in, north_courant_in, obs_cell_in, obs_value_in, obs_error_var_in,
    loc_lat, loc_lon_in, adv_out, prior_out, obs_terms, pair_weights, cell_weights, overflow,
    east_courant, north_courant, obs_cell, obs_value, obs_error_var, loc_lon, small_sem,
    cells_in, from_north, from_south, edge_out, edge_in, lat_own, lat_in, lon_in,
    load_sem, halo_send, halo_recv, lat_send, lat_recv, lon_send, lon_recv,
):
    la, lo = lax.axis_index("lat"), lax.axis_index("lon")

    def at(dlat, dlon):
        return ((la + dlat) & (lats - 1), (lo + dlon) & (lons - 1))

    lat_steps = [4, 3, 5, 2, 6, 1, 7]
    lon_steps = [4, -4, 3, -3, 2, -2, 1, -1]

    def prior_rows(d):
        return packed_room * min(reach + 1 - abs(d), batches)

    barrier = pltpu.get_barrier_semaphore()
    loads = [
        [
            pltpu.make_async_copy(
                state.at[:, k, r, :], cells_in.at[k * rows + r], load_sem.at[k * rows + r]
            )
            for r in range(rows)
        ]
        for k in range(channels)
    ]
    pairs = [
        (obs_cell_in, obs_cell), (east_courant_in, east_courant),
        (north_courant_in, north_courant), (obs_value_in, obs_value),
        (obs_error_var_in, obs_error_var), (loc_lon_in, loc_lon),
    ]
    small = [
        pltpu.make_async_copy(src, dst, small_sem.at[i]) for i, (src, dst) in enumerate(pairs)
    ]
    for load in loads[0] + small + loads[1] + loads[2]:
        load.start()
    peers = [at(1, 0), at(-1, 0), at(0, 1), at(0, -1)]
    peers += [at(d, 0) for d in lat_steps[:-2]] + [at(0, d) for d in lon_steps[:-2]]
    for peer in peers:
        pl.semaphore_signal(barrier, inc=1, device_id=peer, device_id_type=mesh_ids)
    for d in lon_steps:
        unsent = packed_room * batches - prior_rows(d)
        if unsent:
            lon_in[reach - d, prior_rows(d) :] = jnp.zeros((unsent, cols), jnp.float32)
    lane = iota((members, cols), 1)

    def pack_edges(k):
        for side, column in ((0, 0), (1, cols - 1)):
            packed = jnp.zeros((members, cols), jnp.float32)
            for r in range(rows):
                edge = cells_in[k * rows + r, :, column : column + 1]
                packed = jnp.where(lane == r, edge, packed)
            edge_out[side, k] = packed

    def halo_copies(first, count, base):
        made = []
        sends = [
            (cells_in.at[first * rows], from_north.at[first], at(-1, 0)),
            (cells_in.at[first * rows + rows - 1], from_south.at[first], at(1, 0)),
            (edge_out.at[1, first], edge_in.at[0, first], at(0, 1)),
            (edge_out.at[0, first], edge_in.at[1, first], at(0, -1)),
        ]
        for i, (src, dst, peer) in enumerate(sends):
            made.append(
                pltpu.make_async_remote_copy(
                    src_ref=src, dst_ref=dst, send_sem=halo_send.at[base + i],
                    recv_sem=halo_recv.at[base + i], device_id=peer, device_id_type=mesh_ids,
                )
            )
        return made

    for load in loads[0]:
        load.wait()
    pack_edges(0)
    pl.semaphore_wait(barrier, len(peers))
    halos = [halo_copies(k, 1, 4 * k) for k in range(channels)]
    for copy in halos[0]:
        copy.start()

    for load in small:
        load.wait()

    lat_tile, row, lon_tile, col = place(obs_cell[...])
    mine = [lon_tile[b : b + 1] == lo for b in range(batches)]
    tile = (la - iota((lats, batch_obs), 0)) & (lats - 1)
    marks = [one_hot((lat_tile[b : b + 1] == tile) & mine[b]) for b in range(batches)]
    counts = earlier_counts(jnp.concatenate(marks, axis=0))
    base = jnp.zeros((lats, 1), jnp.float32)
    tile_slot, col_slot = [], []
    for b in range(batches):
        before = counts[b * lats : (b + 1) * lats]
        tile_slot.append(jnp.where(marks[b] > 0, before + base, -1.0))
        col_slot.append(jnp.where(mine[b], jnp.sum(before, axis=0, keepdims=True), -1.0))
        base = base + jnp.sum(marks[b], axis=1, keepdims=True)
    slot_ids = iota((tile_room, batch_obs), 0).astype(jnp.float32)
    in_slot = [
        [one_hot(tile_slot[b][d : d + 1] == slot_ids).astype(jnp.bfloat16) for d in range(lats)]
        for b in range(batches)
    ]
    found = jnp.zeros((tile_room, 8), jnp.float32)
    for b in range(batches):
        kinds = iota((8, batch_obs), 0)
        facts = jnp.where(
            kinds == 0,
            row[b : b + 1],
            jnp.where(kinds == 1, col[b : b + 1], jnp.where(kinds == 2, 1, 0)),
        ).astype(jnp.float32).astype(jnp.bfloat16)
        found = found + dot_t(in_slot[b][0], facts)
    slot_row = jnp.where(found[:, 2:3] > 0.5, found[:, 0:1], -1.0)
    slot_col = found[:, 1:2]

    col_ids = iota((room, batch_obs), 0).astype(jnp.float32)
    moves = []
    for b in range(batches):
        wanted = one_hot(col_slot[b] == col_ids).astype(jnp.bfloat16)
        moves.append(dot_t(wanted, jnp.concatenate(in_slot[b], axis=0)))
    move = jnp.concatenate(moves, axis=0)

    inverse_error = 1.0 / obs_error_var[...]
    value_term = obs_value[...] * inverse_error
    lon_table = column_weights(loc_lon)
    lanes = iota((1, cols), 1)
    tiles = (lo - reach + iota((16, batch_obs), 0)) & (lons - 1)
    marks = [one_hot(lon_tile[b : b + 1] == tiles) for b in range(batches)]
    counts = earlier_counts(jnp.concatenate(marks, axis=0))
    row_ids, lon_of, col_hot, row_hot, lat_of = [], [], [], [], []
    kinds = iota((8, batch_obs), 0)

    def describe(b):
        taken = jnp.where(marks[b] > 0, counts[16 * b : 16 * b + 16], -1.0)
        hot = jnp.concatenate(
            [
                one_hot(taken[reach + k : reach + k + 1] == slot_ids)
                for k in range(-spans[b], spans[b] + 1)
            ],
            axis=0,
        )
        one = slice(b, b + 1)
        whole_row = (lat_tile[one] * rows + row[one]).astype(jnp.float32)
        facts = jnp.where(kinds == 0, inverse_error[one], 0.0)
        facts = jnp.where(kinds == 1, value_term[one], facts)
        facts = jnp.where(kinds == 2, col[one].astype(jnp.float32), facts)
        facts = jnp.where(kinds == 3, whole_row, facts)
        facts = jnp.where(kinds == 4, 1.0, facts)
        found = dot_t(hot, facts, highest)
        obs_terms[rows_of(b), :] = found
        at_col = jnp.where(found[:, 4:5] > 0.5, found[:, 2:3], -1.0).astype(jnp.int32)
        at_row = found[:, 3:4].astype(jnp.int32)
        row_ids.append(at_row)
        col_hot.append(one_hot(at_col == lanes))
        row_hot.append(one_hot(at_row == lanes))
        lon_of.append(
            jnp.dot(
                col_hot[b], lon_table, precision=highest, preferred_element_type=jnp.float32
            )
        )
        lat_of.append(lat_weight(at_row - lanes, loc_lat))

    describe(0)

    def advect(k):
        no_north, no_south = la == lats - 1, la == 0
        for r in range(rows):
            here = cells_in[k * rows + r]
            if r + 1 < rows:
                north = cells_in[k * rows + r + 1]
            else:
                north = jnp.where(no_north, 0.0, from_north[k])
            if r > 0:
                south = cells_in[k * rows + r - 1]
            else:
                south = jnp.where(no_south, 0.0, from_south[k])
            adv_out[k * rows + r] = advect_row(
                here, north, south, edge_in[0, k, :, r : r + 1], edge_in[1, k, :, r : r + 1],
                east_courant[r : r + 1, :], north_courant[r : r + 1, :],
            )

    for copy in halos[0]:
        copy.wait_recv()
    advect(0)
    spot = iota((tile_room, cols), 1).astype(jnp.float32)
    picked = jnp.zeros((tile_room, members), jnp.float32)
    for r in range(rows):
        chosen = one_hot((slot_col == spot) & (slot_row == r))
        picked = picked + dot_t(chosen, adv_out[r], highest)
    picked = jnp.concatenate(
        [picked, jnp.zeros((tile_room, cols - members), jnp.float32)], axis=1
    )
    lat_own[...] = packed(picked)
    lat_copies = []
    for d in lat_steps:
        copy = pltpu.make_async_remote_copy(
            src_ref=lat_own, dst_ref=lat_in.at[d - 1], send_sem=lat_send.at[d - 1],
            recv_sem=lat_recv.at[d - 1], device_id=at(d, 0), device_id_type=mesh_ids,
        )
        copy.start()
        lat_copies.append(copy)

    for k in range(1, channels):
        for load in loads[k]:
            load.wait()
        pack_edges(k)
        for copy in halos[k]:
            copy.start()
    for b in range(1, batches):
        describe(b)

    def lon_field(b, k):
        return jnp.concatenate(
            [
                lon_of[b][block(b, k - 1), 2 * cols : 3 * cols],
                lon_of[b][block(b, k), cols : 2 * cols],
                lon_of[b][block(b, k + 1), :cols],
            ],
            axis=0,
        )

    unused = jnp.zeros((cols - 3 * room, cols), jnp.float32)

    for copy in lat_copies:
        copy.wait_recv()
    parts = [unpacked(lat_own[...])] + [unpacked(lat_in[d]) for d in range(lats - 1)]
    parts = jnp.concatenate(parts, axis=0)
    column = jnp.dot(move, parts, precision=highest, preferred_element_type=jnp.float32)
    for b in range(batches):
        lon_in[reach, packed_room * b : packed_room * (b + 1)] = packed(
            column[room * b : room * (b + 1)]
        )
    lon_copies = []
    for i, d in enumerate(lon_steps):
        part = pl.ds(0, prior_rows(d))
        copy = pltpu.make_async_remote_copy(
            src_ref=lon_in.at[reach, part], dst_ref=lon_in.at[reach - d, part],
            send_sem=lon_send.at[i], recv_sem=lon_recv.at[i],
            device_id=at(0, d), device_id_type=mesh_ids,
        )
        copy.start()
        lon_copies.append(copy)
    for k in range(1, channels):
        for copy in halos[k]:
            copy.wait_recv()
        advect(k)

    for (b, k), i in pair_ids.items():
        later = later_batches(b, k)
        cols_t = jnp.concatenate([col_hot[c][block(c, k)] for c in later], axis=0)
        rows_t = jnp.concatenate([row_hot[c][block(c, k)] for c in later], axis=0)
        by_lon = jnp.concatenate([lon_field(b, k), unused], axis=0)
        by_lat = jnp.concatenate([lat_of[b][around(k, b)], unused], axis=0)
        pair_weights[i, : pair_rows(b, k)] = dot_t(cols_t, by_lon, highest) * dot_t(
            rows_t, by_lat, highest
        )
    for b in range(batches):
        weights = lon_field(b, 0)
        for r in range(rows):
            gap = row_ids[b][around(0, b)] - (la * rows + r)
            cell_weights[b, r] = lat_weight(gap, loc_lat) * weights
    in_tile = jnp.zeros((lats, lons), jnp.float32)
    too_many = jnp.zeros((1, lons), jnp.float32)
    for b in range(batches):
        by_lat = one_hot(lat_tile[b : b + 1] == iota((lats, batch_obs), 0))
        by_lon = one_hot(lon_tile[b : b + 1] == iota((lons, batch_obs), 0))
        tally = dot_t(by_lat.astype(jnp.bfloat16), by_lon.astype(jnp.bfloat16))
        in_tile = in_tile + tally
        too_many = jnp.maximum(too_many, jnp.sum(tally, axis=0, keepdims=True) - room)
    too_many = jnp.maximum(too_many, jnp.max(in_tile, axis=0, keepdims=True) - tile_room)
    overflow[0, 0] = jnp.max(too_many).astype(jnp.int32)
    for copy in lon_copies:
        copy.wait_recv()
    prior_out[...] = lon_in[...]
    for copies in (*halos, lat_copies, lon_copies):
        for copy in copies:
            copy.wait_send()


def exchange(
    state, east_courant, north_courant, obs_cell, obs_value, obs_error_var, loc_lat, loc_lon
):
    vmem = pl.BlockSpec(memory_space=pltpu.VMEM)
    smem = pl.BlockSpec(memory_space=pltpu.SMEM)
    f32 = jnp.float32
    slots = packed_room * batches
    return pl.pallas_call(
        exchange_kernel,
        name="exchange",
        out_shape=(
            jax.ShapeDtypeStruct((channels * rows, members, cols), f32),
            jax.ShapeDtypeStruct((2 * reach + 1, slots, cols), f32),
            jax.ShapeDtypeStruct((rows_of(batches - 1).stop, 8), f32),
            jax.ShapeDtypeStruct((len(pair_ids), 3 * room, cols), f32),
            jax.ShapeDtypeStruct((batches, rows, 3 * room, cols), f32),
            jax.ShapeDtypeStruct((1, 1), jnp.int32),
        ),
        in_specs=[pl.BlockSpec(memory_space=pltpu.HBM)] * 6 + [smem, pl.BlockSpec(memory_space=pltpu.HBM)],
        out_specs=(vmem,) * 5 + (smem,),
        scratch_shapes=[
            pltpu.VMEM((rows, cols), f32),
            pltpu.VMEM((rows, cols), f32),
            pltpu.VMEM((batches, batch_obs), jnp.int32),
            pltpu.VMEM((batches, batch_obs), f32),
            pltpu.VMEM((batches, batch_obs), f32),
            pltpu.VMEM((1, cols + 1), f32),
            pltpu.SemaphoreType.DMA((6,)),
            pltpu.VMEM((channels * rows, members, cols), f32),
            pltpu.VMEM((channels, members, cols), f32),
            pltpu.VMEM((channels, members, cols), f32),
            pltpu.VMEM((2, channels, members, cols), f32),
            pltpu.VMEM((2, channels, members, cols), f32),
            pltpu.VMEM((packed_room, cols), f32),
            pltpu.VMEM((lats - 1, packed_room, cols), f32),
            pltpu.VMEM((2 * reach + 1, slots, cols), f32),
            pltpu.SemaphoreType.DMA((channels * rows,)),
            pltpu.SemaphoreType.DMA((4 * channels,)),
            pltpu.SemaphoreType.DMA((4 * channels,)),
            pltpu.SemaphoreType.DMA((lats - 1,)),
            pltpu.SemaphoreType.DMA((lats - 1,)),
            pltpu.SemaphoreType.DMA((2 * reach,)),
            pltpu.SemaphoreType.DMA((2 * reach,)),
        ],
        compiler_params=pltpu.CompilerParams(
            collective_id=0, has_side_effects=True, vmem_limit_bytes=24 << 20
        ),
    )(
        state, east_courant, north_courant, obs_cell, obs_value, obs_error_var, loc_lat,
        loc_lon.reshape(1, -1),
    )


def update_kernel(adv, priors, obs_terms, pair_weights, cell_weights, out, field, slots, sem):
    for k in range(-reach, reach + 1):
        for b in range(batches):
            if abs(k) <= spans[b]:
                part = priors[reach + k, packed_room * b : packed_room * (b + 1)]
                slots[reach + k, room * b : room * (b + 1)] = unpacked(part)
    lane = iota((1, cols), 1)
    is_member = lane < members
    unused = jnp.zeros((cols - 3 * room, cols), jnp.float32)
    unused_three = jnp.zeros((cols - 3 * room, 3 * cols), jnp.float32)
    chunk = 4
    copies = []
    for b in range(batches):
        mine = slice(b * room, (b + 1) * room)
        prior = jnp.concatenate(
            [slots[reach + k, mine] for k in range(-spans[b], spans[b] + 1)], axis=0
        )
        mean = jnp.sum(prior, axis=1, keepdims=True) / members
        anomaly = jnp.where(is_member, prior - mean, 0.0)
        variance = (
            jnp.sum(anomaly * anomaly, axis=1, keepdims=True) / (members - 1) + variance_eps
        )
        precision = 1.0 / variance
        post_var = 1.0 / (precision + obs_terms[rows_of(b), 0:1])
        post_mean = post_var * (mean * precision + obs_terms[rows_of(b), 1:2])
        increment = post_mean + jnp.sqrt(post_var * precision) * anomaly - prior
        increment = jnp.where(is_member, increment, 0.0)
        scaled = anomaly * (precision / (members - 1))
        increment_high, increment_low = halves(increment)
        scaled_high, scaled_low = halves(scaled)
        scaled_three = jnp.concatenate([scaled_high, scaled_high, scaled_low], axis=1)
        for k in targets(b):
            first = (b + 1) * room
            size = pair_rows(b, k)
            target = slots[reach + k, first : first + size]
            high, low = halves(target)
            target_three = jnp.concatenate([high, low, high], axis=1).astype(jnp.bfloat16)
            sources = jnp.concatenate([scaled_three[around(k, b)], unused_three], axis=0)
            gain = dot_t(target_three, sources.astype(jnp.bfloat16))
            high, low = halves(gain * pair_weights[pair_ids[b, k], :size])
            gain_three = jnp.concatenate([high, low, high], axis=1).astype(jnp.bfloat16)
            near_high = jnp.concatenate([increment_high[around(k, b)], unused], axis=0)
            near_low = jnp.concatenate([increment_low[around(k, b)], unused], axis=0)
            near_three = jnp.concatenate([near_high, near_high, near_low], axis=0)
            slots[reach + k, first : first + size] = target + dot(
                gain_three, near_three.astype(jnp.bfloat16)
            )
        near = around(0, b)
        none = jnp.zeros((3 * room, cols), jnp.float32)
        high = jnp.concatenate([scaled_high[near], none], axis=1)
        low = jnp.concatenate([scaled_low[near], none], axis=1)
        scaled_by_member = (
            high + pltpu.roll(high, members, 1) + pltpu.roll(low, 2 * members, 1)
        ).astype(jnp.bfloat16)
        increment_by_slot = jnp.concatenate(
            [
                increment_high[near],
                increment_high[near],
                increment_low[near],
                jnp.zeros((2 * cols - 9 * room, cols), jnp.float32),
            ],
            axis=0,
        )
        increment_by_slot = increment_by_slot.T[:members].astype(jnp.bfloat16)
        before = adv if b == 0 else field
        for start in range(0, channels * rows, chunk):
            cells = jnp.concatenate([before[start + i] for i in range(chunk)], axis=1)
            high = cells.astype(jnp.bfloat16)
            low = (cells - high.astype(jnp.float32)).astype(jnp.bfloat16)
            three = jnp.concatenate(
                [high, low, high, jnp.zeros((2 * cols - 3 * members, chunk * cols), jnp.bfloat16)],
                axis=0,
            )
            gain = dot(scaled_by_member, three) * jnp.concatenate(
                [cell_weights[b, (start + i) % rows] for i in range(chunk)], axis=1
            )
            high, low = halves(gain)
            three = jnp.concatenate(
                [high, low, high, jnp.zeros((2 * cols - 9 * room, chunk * cols), jnp.float32)],
                axis=0,
            ).astype(jnp.bfloat16)
            cells = cells + dot(increment_by_slot, three)
            for i in range(chunk):
                field[start + i] = cells[:, i * cols : (i + 1) * cols]
                if b == batches - 1:
                    k, r = divmod(start + i, rows)
                    copy = pltpu.make_async_copy(
                        field.at[start + i], out.at[:, k, r, :], sem.at[start + i]
                    )
                    copy.start()
                    copies.append(copy)
    for copy in copies:
        copy.wait()


def update(*operands):
    vmem = pl.BlockSpec(memory_space=pltpu.VMEM)
    return pl.pallas_call(
        update_kernel,
        name="update",
        out_shape=jax.ShapeDtypeStruct((members, channels, rows, cols), jnp.float32),
        in_specs=[vmem] * 5,
        out_specs=pl.BlockSpec(memory_space=pltpu.HBM),
        scratch_shapes=[
            pltpu.VMEM((channels * rows, members, cols), jnp.float32),
            pltpu.VMEM((2 * reach + 1, room * batches, cols), jnp.float32),
            pltpu.SemaphoreType.DMA((channels * rows,)),
        ],
        compiler_params=pltpu.CompilerParams(vmem_limit_bytes=61 << 20),
    )(*operands)


def on_device(*args):
    *operands, overflow = exchange(*args)
    return lax.cond(
        overflow.reshape(()) > 0,
        lambda args, operands: general(*args),
        lambda args, operands: update(*operands),
        args,
        tuple(operands),
    )


def solution(mesh):
    in_specs = (
        P(None, None, "lat", "lon"),
        P("lat", "lon"),
        P("lat", "lon"),
        P(),
        P(),
        P(),
        P(),
        P(),
    )
    out_specs = P(None, None, "lat", "lon")
    return jax.shard_map(
        on_device, mesh=mesh, in_specs=in_specs, out_specs=out_specs, check_vma=False
    )
```

```python
import functools
import jax
import jax.numpy as jnp
from jax import lax
from jax.experimental import pallas as pl
from jax.experimental.pallas import tpu as pltpu
from jax.sharding import PartitionSpec as P

diffusion_number = 0.2
variance_eps = 1e-06
highest = lax.Precision.HIGHEST
mesh_ids = pl.DeviceIdType.MESH

rows, cols, lats, lons = 8, 128, 8, 32
members, channels, batches, batch_obs = 80, 3, 4, 256
tile_room, room, packed_room = 24, 24, 16
reach = 4


def shifted(value, axis, by, closed):
    count = lax.axis_size(axis)
    pairs = [(i, (i + by) % count) for i in range(count) if closed or 0 <= i + by < count]
    return lax.ppermute(value, axis, pairs)


def padded(cells, axis, dim, closed):
    last = cells.shape[dim] - 1
    head = lax.slice_in_dim(cells, 0, 1, axis=dim)
    tail = lax.slice_in_dim(cells, last, last + 1, axis=dim)
    return jnp.concatenate(
        [shifted(tail, axis, 1, closed), cells, shifted(head, axis, -1, closed)], axis=dim
    )


def obs_increments(priors, values, error_var):
    prior_mean = jnp.mean(priors, axis=0)
    anomaly = priors - prior_mean
    variance = jnp.sum(anomaly * anomaly, axis=0) / (members - 1) + variance_eps
    post_var = 1.0 / (1.0 / variance + 1.0 / error_var)
    post_mean = post_var * (prior_mean / variance + values / error_var)
    return (anomaly, variance, post_mean + jnp.sqrt(post_var / variance) * anomaly - priors)


def collect(local_priors):
    column = (
        local_priors
        + shifted(local_priors, "lat", 1, False)
        + shifted(local_priors, "lat", -1, False)
    )
    return column + shifted(column, "lon", 1, True) + shifted(column, "lon", -1, True)


def looked_up(table, distance):
    steps = jnp.arange(table.shape[0], dtype=jnp.int32)[:, None, None]
    return jnp.sum(jnp.where(distance[None] == steps, table[:, None, None], 0.0), axis=0)


def general(
    state, east_courant, north_courant, obs_cell, obs_value, obs_error_var, loc_lat, loc_lon
):
    tile_rows, tile_cols = state.shape[2:]
    cell_count = tile_rows * tile_cols
    obs_count = obs_cell.shape[1]
    lat_padded = padded(state, "lat", 2, False)
    lon_padded = padded(state, "lon", 3, True)
    north_side = lat_padded[:, :, 2:, :]
    south_side = lat_padded[:, :, :-2, :]
    east_side = lon_padded[:, :, :, 2:]
    west_side = lon_padded[:, :, :, :-2]
    advected = (
        state
        - 0.5 * east_courant * (east_side - west_side)
        - 0.5 * north_courant * (north_side - south_side)
        + diffusion_number * (east_side + west_side + north_side + south_side - 4.0 * state)
    )
    first_row = lax.axis_index("lat") * tile_rows
    first_col = lax.axis_index("lon") * tile_cols
    grid_cols = tile_cols * lax.axis_size("lon")
    row_ids = first_row + jnp.arange(tile_rows, dtype=jnp.int32)
    col_ids = first_col + jnp.arange(tile_cols, dtype=jnp.int32)

    def step(batch, field):
        cells = lax.dynamic_index_in_dim(obs_cell, batch, 0, False)
        values = lax.dynamic_index_in_dim(obs_value, batch, 0, False)
        error_var = lax.dynamic_index_in_dim(obs_error_var, batch, 0, False)
        obs_row, obs_col = cells // grid_cols, cells % grid_cols
        spot = (obs_row - first_row) * tile_cols + obs_col - first_col
        owned = (obs_col >= first_col) & (obs_col < first_col + tile_cols)
        spot = jnp.where(owned, spot, -1)
        chosen = (jnp.arange(cell_count, dtype=jnp.int32)[:, None] == spot[None, :]).astype(
            jnp.float32
        )
        priors = collect(jnp.dot(field[:, :cell_count], chosen, precision=highest))
        lat_dist = jnp.abs(row_ids[None, :] - obs_row[:, None])
        gap = (col_ids[None, :] - obs_col[:, None]) % grid_cols
        lon_dist = jnp.minimum(gap, grid_cols - gap)
        weights = (
            looked_up(loc_lat, lat_dist)[:, :, None] * looked_up(loc_lon, lon_dist)[:, None, :]
        ).reshape(obs_count, cell_count)
        anomaly, variance, increments = obs_increments(priors, values, error_var)
        field_anom = field - jnp.mean(field, axis=0)
        covar = lax.dot_general(
            anomaly, field_anom, (((0,), (0,)), ((), ())), precision=highest
        ) / (members - 1)
        gain = covar * jnp.tile(weights, (1, channels)) / variance[:, None]
        return field + jnp.dot(increments, gain, precision=highest)

    field = lax.fori_loop(0, batches, step, advected.reshape(members, channels * cell_count))
    return field.reshape(state.shape)


def iota(shape, dim):
    return lax.broadcasted_iota(jnp.int32, shape, dim)


def one_hot(condition):
    return condition.astype(jnp.float32)


def dot_t(a, b, precision=None):
    return lax.dot_general(
        a, b, (((1,), (1,)), ((), ())), precision=precision, preferred_element_type=jnp.float32
    )


def dot(a, b):
    return jnp.dot(a, b, preferred_element_type=jnp.float32)


def halves(value):
    high = value.astype(jnp.bfloat16).astype(jnp.float32)
    return high, value - high


def earlier_counts(marks):
    size = marks.shape[1]
    earlier = (iota((size, size), 0) < iota((size, size), 1)).astype(jnp.bfloat16)
    return jnp.dot(marks.astype(jnp.bfloat16), earlier, preferred_element_type=jnp.float32)


def place(cells):
    return cells >> 15, (cells >> 12) & 7, (cells >> 7) & 31, cells & 127


spans = [reach - b for b in range(batches)]


def block(b, k):
    first = (k + spans[b]) * room
    return slice(first, first + room)


def around(k, b):
    first = (k - 1 + spans[b]) * room
    return slice(first, first + 3 * room)


def rows_of(b):
    first = sum(2 * spans[c] + 1 for c in range(b)) * room
    return slice(first, first + (2 * spans[b] + 1) * room)


def targets(b):
    return range(-spans[b] + 1, spans[b]) if b + 1 < batches else ()


def later_batches(b, k):
    return [c for c in range(b + 1, batches) if abs(k) <= spans[c]]


def pair_rows(b, k):
    return room * len(later_batches(b, k))


pair_ids = {
    pair: i for i, pair in enumerate((b, k) for b in range(batches) for k in targets(b))
}


def lat_weight(gap, loc_lat):
    weight = jnp.zeros(gap.shape, jnp.float32)
    for d in range(rows + 1):
        weight = jnp.where(jnp.abs(gap) == d, loc_lat[d], weight)
    return weight


def column_weights(loc_lon):
    wide = (2 * cols, 4 * cols)
    distance = jnp.abs(iota(wide, 1) - 2 * cols)
    table = one_hot(distance == iota(wide, 0))[:cols]
    ends = one_hot(jnp.abs(iota((8, 4 * cols), 1) - 2 * cols) == cols)
    line = jnp.dot(
        jnp.broadcast_to(loc_lon[:, :cols], (8, cols)), table, precision=highest,
        preferred_element_type=jnp.float32,
    ) + ends * loc_lon[:, cols : cols + 1]
    lines = jnp.broadcast_to(line[0:1], (cols, 4 * cols))
    return pltpu.roll(lines, 0, 1, stride=1, stride_axis=0)[:, cols:]


def packed(block):
    lane = iota((8, cols), 1)
    last = block[16:24]
    return jnp.concatenate(
        [
            jnp.where(lane < members, block[:8], pltpu.roll(last, members, 1)),
            jnp.where(lane < members, block[8:16], pltpu.roll(last, 32, 1)),
        ],
        axis=0,
    )


def unpacked(block):
    lane = iota((8, cols), 1)
    first, second = block[:8], block[8:16]
    last = jnp.where(lane < 48, pltpu.roll(first, 48, 1), pltpu.roll(second, 96, 1))
    three = [jnp.where(lane < members, part, 0.0) for part in (first, second, last)]
    return jnp.concatenate(three, axis=0)


def advect_row(here, north, south, west_halo, east_halo, east_courant, north_courant):
    lane = iota(here.shape, 1)
    east = jnp.where(lane == cols - 1, east_halo, pltpu.roll(here, cols - 1, 1))
    west = jnp.where(lane == 0, west_halo, pltpu.roll(here, 1, 1))
    return (
        here
        - 0.5 * east_courant * (east - west)
        - 0.5 * north_courant * (north - south)
        + diffusion_number * (east + west + north + south - 4.0 * here)
    )


def exchange_kernel(
    state, east_courant_in, north_courant_in, obs_cell_in, obs_value_in, obs_error_var_in,
    loc_lat, loc_lon_in, adv_out, prior_out, obs_terms, pair_weights, cell_weights, overflow,
    east_courant, north_courant, obs_cell, obs_value, obs_error_var, loc_lon, small_sem,
    cells_in, from_north, from_south, edge_out, edge_in, lat_own, lat_in, lon_in,
    load_sem, halo_send, halo_recv, lat_send, lat_recv, lon_send, lon_recv,
):
    la, lo = lax.axis_index("lat"), lax.axis_index("lon")

    def at(dlat, dlon):
        return ((la + dlat) & (lats - 1), (lo + dlon) & (lons - 1))

    lat_steps = [4, 3, 5, 2, 6, 1, 7]
    lon_steps = [4, -4, 3, -3, 2, -2, 1, -1]

    def prior_rows(d):
        return packed_room * min(reach + 1 - abs(d), batches)

    barrier = pltpu.get_barrier_semaphore()
    loads = [
        [
            pltpu.make_async_copy(
                state.at[:, k, r, :], cells_in.at[k * rows + r], load_sem.at[k * rows + r]
            )
            for r in range(rows)
        ]
        for k in range(channels)
    ]
    pairs = [
        (obs_cell_in, obs_cell), (east_courant_in, east_courant),
        (north_courant_in, north_courant), (obs_value_in, obs_value),
        (obs_error_var_in, obs_error_var), (loc_lon_in, loc_lon),
    ]
    small = [
        pltpu.make_async_copy(src, dst, small_sem.at[i]) for i, (src, dst) in enumerate(pairs)
    ]
    for load in loads[0] + small + loads[1] + loads[2]:
        load.start()
    peers = [at(1, 0), at(-1, 0), at(0, 1), at(0, -1)]
    peers += [at(d, 0) for d in lat_steps[:-2]] + [at(0, d) for d in lon_steps[:-2]]
    for peer in peers:
        pl.semaphore_signal(barrier, inc=1, device_id=peer, device_id_type=mesh_ids)
    for d in lon_steps:
        unsent = packed_room * batches - prior_rows(d)
        if unsent:
            lon_in[reach - d, prior_rows(d) :] = jnp.zeros((unsent, cols), jnp.float32)
    lane = iota((members, cols), 1)

    def pack_edges(k):
        for side, column in ((0, 0), (1, cols - 1)):
            packed = jnp.zeros((members, cols), jnp.float32)
            for r in range(rows):
                edge = cells_in[k * rows + r, :, column : column + 1]
                packed = jnp.where(lane == r, edge, packed)
            edge_out[side, k] = packed

    def halo_copies(first, count, base):
        made = []
        sends = [
            (cells_in.at[first * rows], from_north.at[first], at(-1, 0)),
            (cells_in.at[first * rows + rows - 1], from_south.at[first], at(1, 0)),
            (edge_out.at[1, first], edge_in.at[0, first], at(0, 1)),
            (edge_out.at[0, first], edge_in.at[1, first], at(0, -1)),
        ]
        for i, (src, dst, peer) in enumerate(sends):
            made.append(
                pltpu.make_async_remote_copy(
                    src_ref=src, dst_ref=dst, send_sem=halo_send.at[base + i],
                    recv_sem=halo_recv.at[base + i], device_id=peer, device_id_type=mesh_ids,
                )
            )
        return made

    for load in loads[0]:
        load.wait()
    pack_edges(0)
    pl.semaphore_wait(barrier, len(peers))
    halos = [halo_copies(k, 1, 4 * k) for k in range(channels)]
    for copy in halos[0]:
        copy.start()

    for load in small:
        load.wait()

    lat_tile, row, lon_tile, col = place(obs_cell[...])
    mine = [lon_tile[b : b + 1] == lo for b in range(batches)]
    tile = (la - iota((lats, batch_obs), 0)) & (lats - 1)
    marks = [one_hot((lat_tile[b : b + 1] == tile) & mine[b]) for b in range(batches)]
    counts = earlier_counts(jnp.concatenate(marks, axis=0))
    base = jnp.zeros((lats, 1), jnp.float32)
    tile_slot, col_slot = [], []
    for b in range(batches):
        before = counts[b * lats : (b + 1) * lats]
        tile_slot.append(jnp.where(marks[b] > 0, before + base, -1.0))
        col_slot.append(jnp.where(mine[b], jnp.sum(before, axis=0, keepdims=True), -1.0))
        base = base + jnp.sum(marks[b], axis=1, keepdims=True)
    slot_ids = iota((tile_room, batch_obs), 0).astype(jnp.float32)
    in_slot = [
        [one_hot(tile_slot[b][d : d + 1] == slot_ids).astype(jnp.bfloat16) for d in range(lats)]
        for b in range(batches)
    ]
    found = jnp.zeros((tile_room, 8), jnp.float32)
    for b in range(batches):
        kinds = iota((8, batch_obs), 0)
        facts = jnp.where(
            kinds == 0,
            row[b : b + 1],
            jnp.where(kinds == 1, col[b : b + 1], jnp.where(kinds == 2, 1, 0)),
        ).astype(jnp.float32).astype(jnp.bfloat16)
        found = found + dot_t(in_slot[b][0], facts)
    slot_row = jnp.where(found[:, 2:3] > 0.5, found[:, 0:1], -1.0)
    slot_col = found[:, 1:2]

    col_ids = iota((room, batch_obs), 0).astype(jnp.float32)
    moves = []
    for b in range(batches):
        wanted = one_hot(col_slot[b] == col_ids).astype(jnp.bfloat16)
        moves.append(dot_t(wanted, jnp.concatenate(in_slot[b], axis=0)))
    move = jnp.concatenate(moves, axis=0)

    inverse_error = 1.0 / obs_error_var[...]
    value_term = obs_value[...] * inverse_error
    lon_table = column_weights(loc_lon)
    lanes = iota((1, cols), 1)
    tiles = (lo - reach + iota((16, batch_obs), 0)) & (lons - 1)
    marks = [one_hot(lon_tile[b : b + 1] == tiles) for b in range(batches)]
    counts = earlier_counts(jnp.concatenate(marks, axis=0))
    row_ids, lon_of, col_hot, row_hot, lat_of = [], [], [], [], []
    kinds = iota((8, batch_obs), 0)

    def describe(b):
        taken = jnp.where(marks[b] > 0, counts[16 * b : 16 * b + 16], -1.0)
        hot = jnp.concatenate(
            [
                one_hot(taken[reach + k : reach + k + 1] == slot_ids)
                for k in range(-spans[b], spans[b] + 1)
            ],
            axis=0,
        )
        one = slice(b, b + 1)
        whole_row = (lat_tile[one] * rows + row[one]).astype(jnp.float32)
        facts = jnp.where(kinds == 0, inverse_error[one], 0.0)
        facts = jnp.where(kinds == 1, value_term[one], facts)
        facts = jnp.where(kinds == 2, col[one].astype(jnp.float32), facts)
        facts = jnp.where(kinds == 3, whole_row, facts)
        facts = jnp.where(kinds == 4, 1.0, facts)
        found = dot_t(hot, facts, highest)
        obs_terms[rows_of(b), :] = found
        at_col = jnp.where(found[:, 4:5] > 0.5, found[:, 2:3], -1.0).astype(jnp.int32)
        at_row = found[:, 3:4].astype(jnp.int32)
        row_ids.append(at_row)
        col_hot.append(one_hot(at_col == lanes))
        row_hot.append(one_hot(at_row == lanes))
        lon_of.append(
            jnp.dot(
                col_hot[b], lon_table, precision=highest, preferred_element_type=jnp.float32
            )
        )
        lat_of.append(lat_weight(at_row - lanes, loc_lat))

    describe(0)

    def advect(k):
        no_north, no_south = la == lats - 1, la == 0
        for r in range(rows):
            here = cells_in[k * rows + r]
            if r + 1 < rows:
                north = cells_in[k * rows + r + 1]
            else:
                north = jnp.where(no_north, 0.0, from_north[k])
            if r > 0:
                south = cells_in[k * rows + r - 1]
            else:
                south = jnp.where(no_south, 0.0, from_south[k])
            adv_out[k * rows + r] = advect_row(
                here, north, south, edge_in[0, k, :, r : r + 1], edge_in[1, k, :, r : r + 1],
                east_courant[r : r + 1, :], north_courant[r : r + 1, :],
            )

    spot = iota((tile_room, cols), 1).astype(jnp.float32)
    in_col = slot_col == spot
    nothing = jnp.zeros((members, cols), jnp.float32)
    picked = jnp.zeros((tile_room, members), jnp.float32)
    winds = jnp.zeros((tile_room, cols), jnp.float32)
    for r in range(rows):
        chosen = one_hot(in_col & (slot_row == r))
        winds = winds + chosen * east_courant[r : r + 1, :]
        inside = advect_row(
            cells_in[r], cells_in[r + 1] if r + 1 < rows else nothing,
            cells_in[r - 1] if r > 0 else nothing, 0.0, 0.0,
            east_courant[r : r + 1, :], north_courant[r : r + 1, :],
        )
        picked = picked + dot_t(chosen, inside, highest)
    wind = jnp.sum(winds, axis=1, keepdims=True)
    last_row = one_hot(in_col & (slot_row == rows - 1) & (la < lats - 1))
    first_row = one_hot(in_col & (slot_row == 0) & (la > 0))
    to_north = last_row * (diffusion_number - 0.5 * north_courant[rows - 1 : rows, :])
    to_south = first_row * (diffusion_number + 0.5 * north_courant[0:1, :])
    to_east = one_hot((slot_row == spot) & (slot_col == cols - 1))
    to_east = to_east * (diffusion_number - 0.5 * wind)
    to_west = one_hot((slot_row == spot) & (slot_col == 0)) * (diffusion_number + 0.5 * wind)
    for copy in halos[0]:
        copy.wait_recv()
    beyond = [
        (to_north, from_north[0]), (to_south, from_south[0]),
        (to_east, edge_in[1, 0]), (to_west, edge_in[0, 0]),
    ]
    for shares, values in beyond:
        picked = picked + dot_t(shares, values, highest)
    picked = jnp.concatenate(
        [picked, jnp.zeros((tile_room, cols - members), jnp.float32)], axis=1
    )
    lat_own[...] = packed(picked)
    lat_copies = []
    for d in lat_steps:
        copy = pltpu.make_async_remote_copy(
            src_ref=lat_own, dst_ref=lat_in.at[d - 1], send_sem=lat_send.at[d - 1],
            recv_sem=lat_recv.at[d - 1], device_id=at(d, 0), device_id_type=mesh_ids,
        )
        copy.start()
        lat_copies.append(copy)

    advect(0)
    for k in range(1, channels):
        for load in loads[k]:
            load.wait()
        pack_edges(k)
        for copy in halos[k]:
            copy.start()
    for b in range(1, batches):
        describe(b)

    def lon_field(b, k):
        return jnp.concatenate(
            [
                lon_of[b][block(b, k - 1), 2 * cols : 3 * cols],
                lon_of[b][block(b, k), cols : 2 * cols],
                lon_of[b][block(b, k + 1), :cols],
            ],
            axis=0,
        )

    unused = jnp.zeros((cols - 3 * room, cols), jnp.float32)

    for copy in lat_copies:
        copy.wait_recv()
    parts = [unpacked(lat_own[...])] + [unpacked(lat_in[d]) for d in range(lats - 1)]
    parts = jnp.concatenate(parts, axis=0)
    column = jnp.dot(move, parts, precision=highest, preferred_element_type=jnp.float32)
    for b in range(batches):
        lon_in[reach, packed_room * b : packed_room * (b + 1)] = packed(
            column[room * b : room * (b + 1)]
        )
    lon_copies = []
    for i, d in enumerate(lon_steps):
        part = pl.ds(0, prior_rows(d))
        copy = pltpu.make_async_remote_copy(
            src_ref=lon_in.at[reach, part], dst_ref=lon_in.at[reach - d, part],
            send_sem=lon_send.at[i], recv_sem=lon_recv.at[i],
            device_id=at(0, d), device_id_type=mesh_ids,
        )
        copy.start()
        lon_copies.append(copy)
    for k in range(1, channels):
        for copy in halos[k]:
            copy.wait_recv()
        advect(k)

    for (b, k), i in pair_ids.items():
        later = later_batches(b, k)
        cols_t = jnp.concatenate([col_hot[c][block(c, k)] for c in later], axis=0)
        rows_t = jnp.concatenate([row_hot[c][block(c, k)] for c in later], axis=0)
        by_lon = jnp.concatenate([lon_field(b, k), unused], axis=0)
        by_lat = jnp.concatenate([lat_of[b][around(k, b)], unused], axis=0)
        pair_weights[i, : pair_rows(b, k)] = dot_t(cols_t, by_lon, highest) * dot_t(
            rows_t, by_lat, highest
        )
    for b in range(batches):
        weights = lon_field(b, 0)
        for r in range(rows):
            gap = row_ids[b][around(0, b)] - (la * rows + r)
            cell_weights[b, r] = lat_weight(gap, loc_lat) * weights
    in_tile = jnp.zeros((lats, lons), jnp.float32)
    too_many = jnp.zeros((1, lons), jnp.float32)
    for b in range(batches):
        by_lat = one_hot(lat_tile[b : b + 1] == iota((lats, batch_obs), 0))
        by_lon = one_hot(lon_tile[b : b + 1] == iota((lons, batch_obs), 0))
        tally = dot_t(by_lat.astype(jnp.bfloat16), by_lon.astype(jnp.bfloat16))
        in_tile = in_tile + tally
        too_many = jnp.maximum(too_many, jnp.sum(tally, axis=0, keepdims=True) - room)
    too_many = jnp.maximum(too_many, jnp.max(in_tile, axis=0, keepdims=True) - tile_room)
    overflow[0, 0] = jnp.max(too_many).astype(jnp.int32)
    for copy in lon_copies:
        copy.wait_recv()
    prior_out[...] = lon_in[...]
    for copies in (*halos, lat_copies, lon_copies):
        for copy in copies:
            copy.wait_send()


def exchange(
    state, east_courant, north_courant, obs_cell, obs_value, obs_error_var, loc_lat, loc_lon
):
    vmem = pl.BlockSpec(memory_space=pltpu.VMEM)
    smem = pl.BlockSpec(memory_space=pltpu.SMEM)
    f32 = jnp.float32
    slots = packed_room * batches
    return pl.pallas_call(
        exchange_kernel,
        name="exchange",
        out_shape=(
            jax.ShapeDtypeStruct((channels * rows, members, cols), f32),
            jax.ShapeDtypeStruct((2 * reach + 1, slots, cols), f32),
            jax.ShapeDtypeStruct((rows_of(batches - 1).stop, 8), f32),
            jax.ShapeDtypeStruct((len(pair_ids), 3 * room, cols), f32),
            jax.ShapeDtypeStruct((batches, rows, 3 * room, cols), f32),
            jax.ShapeDtypeStruct((1, 1), jnp.int32),
        ),
        in_specs=[pl.BlockSpec(memory_space=pltpu.HBM)] * 6 + [smem, pl.BlockSpec(memory_space=pltpu.HBM)],
        out_specs=(vmem,) * 5 + (smem,),
        scratch_shapes=[
            pltpu.VMEM((rows, cols), f32),
            pltpu.VMEM((rows, cols), f32),
            pltpu.VMEM((batches, batch_obs), jnp.int32),
            pltpu.VMEM((batches, batch_obs), f32),
            pltpu.VMEM((batches, batch_obs), f32),
            pltpu.VMEM((1, cols + 1), f32),
            pltpu.SemaphoreType.DMA((6,)),
            pltpu.VMEM((channels * rows, members, cols), f32),
            pltpu.VMEM((channels, members, cols), f32),
            pltpu.VMEM((channels, members, cols), f32),
            pltpu.VMEM((2, channels, members, cols), f32),
            pltpu.VMEM((2, channels, members, cols), f32),
            pltpu.VMEM((packed_room, cols), f32),
            pltpu.VMEM((lats - 1, packed_room, cols), f32),
            pltpu.VMEM((2 * reach + 1, slots, cols), f32),
            pltpu.SemaphoreType.DMA((channels * rows,)),
            pltpu.SemaphoreType.DMA((4 * channels,)),
            pltpu.SemaphoreType.DMA((4 * channels,)),
            pltpu.SemaphoreType.DMA((lats - 1,)),
            pltpu.SemaphoreType.DMA((lats - 1,)),
            pltpu.SemaphoreType.DMA((2 * reach,)),
            pltpu.SemaphoreType.DMA((2 * reach,)),
        ],
        compiler_params=pltpu.CompilerParams(
            collective_id=0, has_side_effects=True, vmem_limit_bytes=24 << 20
        ),
    )(
        state, east_courant, north_courant, obs_cell, obs_value, obs_error_var, loc_lat,
        loc_lon.reshape(1, -1),
    )


def update_kernel(adv, priors, obs_terms, pair_weights, cell_weights, out, field, slots, sem):
    for k in range(-reach, reach + 1):
        for b in range(batches):
            if abs(k) <= spans[b]:
                part = priors[reach + k, packed_room * b : packed_room * (b + 1)]
                slots[reach + k, room * b : room * (b + 1)] = unpacked(part)
    lane = iota((1, cols), 1)
    is_member = lane < members
    unused = jnp.zeros((cols - 3 * room, cols), jnp.float32)
    unused_three = jnp.zeros((cols - 3 * room, 3 * cols), jnp.float32)
    chunk = 24
    copies = []
    for b in range(batches):
        mine = slice(b * room, (b + 1) * room)
        prior = jnp.concatenate(
            [slots[reach + k, mine] for k in range(-spans[b], spans[b] + 1)], axis=0
        )
        mean = jnp.sum(prior, axis=1, keepdims=True) / members
        anomaly = jnp.where(is_member, prior - mean, 0.0)
        variance = (
            jnp.sum(anomaly * anomaly, axis=1, keepdims=True) / (members - 1) + variance_eps
        )
        precision = 1.0 / variance
        post_var = 1.0 / (precision + obs_terms[rows_of(b), 0:1])
        post_mean = post_var * (mean * precision + obs_terms[rows_of(b), 1:2])
        increment = post_mean + jnp.sqrt(post_var * precision) * anomaly - prior
        increment = jnp.where(is_member, increment, 0.0)
        scaled = anomaly * (precision / (members - 1))
        increment_high, increment_low = halves(increment)
        scaled_high, scaled_low = halves(scaled)
        scaled_three = jnp.concatenate([scaled_high, scaled_high, scaled_low], axis=1)
        for k in targets(b):
            first = (b + 1) * room
            size = pair_rows(b, k)
            target = slots[reach + k, first : first + size]
            high, low = halves(target)
            target_three = jnp.concatenate([high, low, high], axis=1).astype(jnp.bfloat16)
            sources = jnp.concatenate([scaled_three[around(k, b)], unused_three], axis=0)
            gain = dot_t(target_three, sources.astype(jnp.bfloat16))
            high, low = halves(gain * pair_weights[pair_ids[b, k], :size])
            gain_three = jnp.concatenate([high, low, high], axis=1).astype(jnp.bfloat16)
            near_high = jnp.concatenate([increment_high[around(k, b)], unused], axis=0)
            near_low = jnp.concatenate([increment_low[around(k, b)], unused], axis=0)
            near_three = jnp.concatenate([near_high, near_high, near_low], axis=0)
            slots[reach + k, first : first + size] = target + dot(
                gain_three, near_three.astype(jnp.bfloat16)
            )
        near = around(0, b)
        none = jnp.zeros((3 * room, cols), jnp.float32)
        high = jnp.concatenate([scaled_high[near], none], axis=1)
        low = jnp.concatenate([scaled_low[near], none], axis=1)
        scaled_by_member = (
            high + pltpu.roll(high, members, 1) + pltpu.roll(low, 2 * members, 1)
        ).astype(jnp.bfloat16)
        increment_by_slot = jnp.concatenate(
            [
                increment_high[near],
                increment_high[near],
                increment_low[near],
                jnp.zeros((2 * cols - 9 * room, cols), jnp.float32),
            ],
            axis=0,
        )
        increment_by_slot = increment_by_slot.T[:members].astype(jnp.bfloat16)
        before = adv if b == 0 else field
        for start in range(0, channels * rows, chunk):
            cells = jnp.concatenate([before[start + i] for i in range(chunk)], axis=1)
            high = cells.astype(jnp.bfloat16)
            low = (cells - high.astype(jnp.float32)).astype(jnp.bfloat16)
            three = jnp.concatenate(
                [high, low, high, jnp.zeros((2 * cols - 3 * members, chunk * cols), jnp.bfloat16)],
                axis=0,
            )
            gain = dot(scaled_by_member, three) * jnp.concatenate(
                [cell_weights[b, (start + i) % rows] for i in range(chunk)], axis=1
            )
            high, low = halves(gain)
            three = jnp.concatenate(
                [high, low, high, jnp.zeros((2 * cols - 9 * room, chunk * cols), jnp.float32)],
                axis=0,
            ).astype(jnp.bfloat16)
            cells = cells + dot(increment_by_slot, three)
            for i in range(chunk):
                field[start + i] = cells[:, i * cols : (i + 1) * cols]
                if b == batches - 1:
                    k, r = divmod(start + i, rows)
                    copy = pltpu.make_async_copy(
                        field.at[start + i], out.at[:, k, r, :], sem.at[start + i]
                    )
                    copy.start()
                    copies.append(copy)
    for copy in copies:
        copy.wait()


def update(*operands):
    vmem = pl.BlockSpec(memory_space=pltpu.VMEM)
    return pl.pallas_call(
        update_kernel,
        name="update",
        out_shape=jax.ShapeDtypeStruct((members, channels, rows, cols), jnp.float32),
        in_specs=[vmem] * 5,
        out_specs=pl.BlockSpec(memory_space=pltpu.HBM),
        scratch_shapes=[
            pltpu.VMEM((channels * rows, members, cols), jnp.float32),
            pltpu.VMEM((2 * reach + 1, room * batches, cols), jnp.float32),
            pltpu.SemaphoreType.DMA((channels * rows,)),
        ],
        compiler_params=pltpu.CompilerParams(vmem_limit_bytes=61 << 20),
    )(*operands)


def on_device(*args):
    *operands, overflow = exchange(*args)
    return lax.cond(
        overflow.reshape(()) > 0,
        lambda args, operands: general(*args),
        lambda args, operands: update(*operands),
        args,
        tuple(operands),
    )


def solution(mesh):
    in_specs = (
        P(None, None, "lat", "lon"),
        P("lat", "lon"),
        P("lat", "lon"),
        P(),
        P(),
        P(),
        P(),
        P(),
    )
    out_specs = P(None, None, "lat", "lon")
    return jax.shard_map(
        on_device, mesh=mesh, in_specs=in_specs, out_specs=out_specs, check_vma=False
    )
```
